32 devices in a mesh: dp: 16 (over z, y, x), tensor: 2 (over core).
Axes of the slice: x: 2, y: 2, z: 4, core: 2. Of those that a mesh axis runs over, the one named last changes fastest.
Arguments:
- latent_x: bfloat16 [1280, 16384], P('tensor', 'dp'), parts along dimension 1, may hold values from -6 to 6
- control_h: bfloat16 [1280, 16384], P('tensor', 'dp'), parts along dimension 1, may hold values from -6 to 6
- tile_mask: int32 [16, 8, 8], P('dp'), parts along dimension 0, may hold values 0 or 1
- timestep: int32 [16], P('dp'), parts along dimension 0, may hold values from 0 to 999
- time_weight: bfloat16 [320, 1280], P(None, 'tensor'), may hold values from -0.5 to 0.5
- norm_gain: float32 [3, 1280], P(None, 'tensor'), may hold values from 0.5 to 1.5
- norm_bias: float32 [3, 1280], P(None, 'tensor'), may hold values from -3 to 3
- unet_conv_in: bfloat16 [9, 1280, 1280], P(None, 'tensor'), may hold values from -0.0546875 to 0.0546875
- unet_conv_out: bfloat16 [9, 1280, 1280], P(None, 'tensor'), may hold values from -0.0546875 to 0.0546875
- control_conv: bfloat16 [9, 1280, 1280], P(None, 'tensor'), may hold values from -0.0546875 to 0.0546875
- unet_temb: bfloat16 [1280, 1280], P('tensor'), may hold values from -0.15625 to 0.15625
- control_temb: bfloat16 [1280, 1280], P('tensor'), may hold values from -0.15625 to 0.15625
- zero_conv: bfloat16 [1280, 1280], P('tensor'), may hold values from -0.15625 to 0.15625
Outputs:
- mixed: bfloat16 [1280, 16384], P('tensor', 'dp'), parts along dimension 1
The draws below stay inside these ranges and needn't reach their ends.
There are 16 independent parts, one for each index of `dp`. The reference program is written for one: setup_inputs(seed, part) draws one part's arguments, and reference() takes and returns one part's arrays. A program takes and returns all parts, laid end to end along the dimension named above; an argument that names none is the same for every part. Nothing has to cross between parts.
All inputs are finite; a program needn't handle non-finite values.
Results may differ from the reference program's by a relative error of at most 0.014.
Values may be sent and summed in bfloat16 or wider, within the bound.
No kernel may reach another device: no remote copies, remote signals or barrier semaphores. Data moves between devices by JAX's collectives and lax.ppermute only.
A program may use at most 192 MiB of HBM per device.

```python
import math
import jax
import jax.numpy as jnp
from jax import lax

C = 1280
GROUPS = 32
FREQ = 320
S = 32
TILE = 4
VIEWS = 1
P_SIZE = 1024


def plant(drawn, stream_key, low, largest):
    spot = [jax.random.randint(jax.random.fold_in(stream_key, axis), (), 0, length) for axis, length in enumerate(drawn.shape)]
    widest = drawn.shape.index(max(drawn.shape))
    next_to = spot[:widest] + [(spot[widest] + 1) % drawn.shape[widest]] + spot[widest + 1:]
    return drawn.at[tuple(spot)].set(low).at[tuple(next_to)].set(largest)


def block_levels(stream_key, extent, split, smallest, largest):
    def one(dim, shards_of):
        steps = jax.random.uniform(jax.random.fold_in(jax.random.fold_in(stream_key, 6), dim), (shards_of,), jnp.float32, smallest / len(split), largest / len(split))
        return jnp.repeat(jnp.exp(steps), extent[dim] // shards_of).reshape((-1,) + (1,) * (len(extent) - dim - 1))

    factor_of = one(*split[0])
    for cut in split[1:]:
        factor_of = factor_of * one(*cut)
    return factor_of


def bell_draw(stream_key, dims, width, most, cuts=(), kind=jnp.bfloat16):
    values = jax.random.normal(stream_key, dims, jnp.float32) * width
    if len(cuts) > 0:
        values = block_levels(stream_key, dims, cuts, -0.22, 0.18) * values
    return jnp.clip(values, min=-most, max=most).astype(kind)


def setup_inputs(seed: int = 0, part: int = 0) -> dict:
    splits = jax.random.split(jax.random.key(seed), 14)
    part_keys = jax.random.split(jax.random.fold_in(splits[13], part), 14)
    return {
        "latent_x": bell_draw(part_keys[0], (C, P_SIZE), 1.0, 6.0, ((0, 2),)),
        "control_h": bell_draw(part_keys[1], (C, P_SIZE), 1.0, 6.0, ((0, 2),)),
        "tile_mask": plant((jax.random.randint(part_keys[2], (VIEWS, S // TILE, S // TILE), 0, 2) < 1).astype(jnp.int32), jax.random.fold_in(part_keys[2], 1), 0, 1),
        "timestep": jax.random.randint(part_keys[3], (1,), 0, 1000).astype(jnp.int32),
        "time_weight": bell_draw(splits[4], (FREQ, C), (FREQ // 2) ** -0.5, 0.5, ((1, 2),)),
        "norm_gain": jnp.clip(1.0 + 0.1 * jax.random.normal(splits[5], (3, C), jnp.float32), 0.5, 1.5),
        "norm_bias": bell_draw(splits[6], (3, C), 0.5, 3.0, ((1, 2),), jnp.float32),
        "unet_conv_in": bell_draw(splits[7], (9, C, C), (9 * C) ** -0.5, 0.0546875, ((1, 2),)),
        "unet_conv_out": bell_draw(splits[8], (9, C, C), (9 * C) ** -0.5, 0.0546875, ((1, 2),)),
        "control_conv": bell_draw(splits[9], (9, C, C), (9 * C) ** -0.5, 0.0546875, ((1, 2),)),
        "unet_temb": bell_draw(splits[10], (C, C), C ** -0.5, 0.15625, ((0, 2),)),
        "control_temb": bell_draw(splits[11], (C, C), C ** -0.5, 0.15625, ((0, 2),)),
        "zero_conv": bell_draw(splits[12], (C, C), C ** -0.5, 0.15625, ((0, 2),)),
    }


def timestep_features(timestep):
    half_width = FREQ // 2
    rates = jnp.exp(-math.log(10000.0) * jnp.arange(half_width, dtype=jnp.float32) / half_width)
    angles = timestep.astype(jnp.float32)[0] * rates
    return jnp.concatenate([jnp.cos(angles), jnp.sin(angles)])

def norm_silu(inputs, scales, shifts):
    rows_count = inputs.shape[0]
    group_size = C // GROUPS
    grouped = inputs.astype(jnp.float32).reshape(rows_count // group_size, group_size, VIEWS, S * S)
    average = lax.optimization_barrier(jnp.mean(grouped, axis=(1, 3), keepdims=True))
    centred = grouped - average
    variance = lax.optimization_barrier(jnp.mean(centred * centred, axis=(1, 3), keepdims=True))
    normed = (centred * lax.rsqrt(variance + 1e-05)).reshape(rows_count, VIEWS * S * S)
    return jax.nn.silu(normed * scales[:, None] + shifts[:, None]).astype(jnp.bfloat16)

def shifted_copies(inputs):
    rows_count = inputs.shape[0]
    picture = inputs.reshape(rows_count, VIEWS, S, S)
    padded = jnp.pad(picture, ((0, 0), (0, 0), (1, 1), (1, 1)))
    copies = []
    for row_step in range(3):
        for col_step in range(3):
            copies.append(padded[:, :, row_step:row_step + S, col_step:col_step + S].reshape(rows_count, VIEWS * S * S))
    return copies

def convolve(inputs, weights, flipped):
    copies = shifted_copies(inputs)
    out_rows = weights.shape[2] if flipped else weights.shape[1]
    result = jnp.zeros((out_rows, inputs.shape[1]), jnp.float32)
    for place in range(9):
        tap = weights[place].T if flipped else weights[place]
        result = result + jnp.dot(tap, copies[place], preferred_element_type=jnp.float32)
    return result

def expand_mask(tile_mask):
    blocks = tile_mask.astype(jnp.float32)[:, :, None, :, None]
    spread_mask = jnp.broadcast_to(blocks, (VIEWS, S // TILE, TILE, S // TILE, TILE))
    return spread_mask.reshape(VIEWS * S * S)

def reference(latent_x, control_h, tile_mask, timestep, time_weight, norm_gain, norm_bias, unet_conv_in, unet_conv_out, control_conv, unet_temb, control_temb, zero_conv):
    time_vector = jax.nn.silu(jnp.dot(timestep_features(timestep), time_weight.astype(jnp.float32), precision=lax.Precision.HIGHEST))
    unet_shift = jnp.dot(unet_temb.astype(jnp.float32), time_vector, precision=lax.Precision.HIGHEST)
    control_shift = jnp.dot(control_temb.astype(jnp.float32), time_vector, precision=lax.Precision.HIGHEST)
    first = norm_silu(latent_x, norm_gain[0], norm_bias[0])
    hidden = (convolve(first, unet_conv_in, False) + unet_shift[:, None]).astype(jnp.bfloat16)
    hidden = lax.optimization_barrier(hidden)
    second = norm_silu(hidden, norm_gain[1], norm_bias[1])
    control_act = norm_silu(control_h, norm_gain[2], norm_bias[2])
    control_state = (control_h.astype(jnp.float32) + convolve(control_act, control_conv, True) + control_shift[:, None]).astype(jnp.bfloat16)
    gate_row = expand_mask(tile_mask)
    residual = jnp.dot(zero_conv.T, control_state, preferred_element_type=jnp.float32) * gate_row[None, :]
    mixed = latent_x.astype(jnp.float32) + convolve(second, unet_conv_out, True) + residual
    return mixed.astype(jnp.bfloat16)
```

```python
import functools
import math

import jax
import jax.numpy as jnp
import numpy as np
from jax import lax
from jax.experimental import pallas as pl
from jax.experimental.pallas import tpu as pltpu
from jax.sharding import PartitionSpec as P

C = 1280
GROUPS = 32
FREQ = 320
S = 32
TILE = 4
VIEWS = 1

BF = jnp.bfloat16
F32 = jnp.float32
WIDE = 256
LANES = 128
CHUNK = 2 * S


def timestep_features(timestep):
    half_width = FREQ // 2
    rates = jnp.exp(-math.log(10000.0) * jnp.arange(half_width, dtype=jnp.float32) / half_width)
    angles = timestep.astype(jnp.float32)[0] * rates
    return jnp.concatenate([jnp.cos(angles), jnp.sin(angles)])


def half_silu(v):
    h = 0.5 * v
    return h + h * jnp.tanh(h)


def group_masks(channels, size):
    groups = channels // size
    row = lax.broadcasted_iota(jnp.int32, (groups, channels), 0)
    col = lax.broadcasted_iota(jnp.int32, (groups, channels), 1)
    return ((col >= row * size) & (col < row * size + size)).astype(F32)


def group_mean(sums, mask, count):
    per_group = jnp.sum(mask * sums, axis=1, keepdims=True) * (1.0 / count)
    return jnp.sum(mask * per_group, axis=0, keepdims=True)


def norm_rows(xt, size, gain):
    cells, channels = xt.shape
    mask = group_masks(channels, size)

    def fold(value):
        return jnp.sum(value.reshape(CHUNK // 8, 8, channels), axis=0)

    def add(i, total):
        return total + fold(xt[pl.ds(pl.multiple_of(i * CHUNK, CHUNK), CHUNK), :].astype(F32))

    total = lax.fori_loop(0, cells // CHUNK, add, jnp.zeros((8, channels), F32))
    mean = group_mean(jnp.sum(total, axis=0, keepdims=True), mask, cells * size)

    def add_square(i, total):
        d = xt[pl.ds(pl.multiple_of(i * CHUNK, CHUNK), CHUNK), :].astype(F32) - mean
        return total + fold(d * d)

    total = lax.fori_loop(0, cells // CHUNK, add_square, jnp.zeros((8, channels), F32))
    variance = group_mean(jnp.sum(total, axis=0, keepdims=True), mask, cells * size)
    return mean, lax.rsqrt(variance + 1e-05) * gain


def turn_in(x_ref, xt):
    channels = x_ref.shape[0]
    for b in range(channels // LANES):
        part = slice(b * LANES, (b + 1) * LANES)
        xt[:, part] = x_ref[part, :].astype(F32).T.astype(BF)


def edge_masks(rows, channels):
    col = lax.broadcasted_iota(jnp.int32, (rows, channels), 0) % S
    return col != 0, col != S - 1


def store_shifted(sh, start, y, left_ok, right_ok, offset=0):
    rows, channels = y.shape
    width = sh.shape[1] // 3
    lo = jnp.where(left_ok, pltpu.roll(y, 1, 0), 0.0)
    hi = jnp.where(right_ok, pltpu.roll(y, rows - 1, 0), 0.0)
    for k, v in enumerate((lo, y, hi)):
        sh[pl.ds(start, rows), k * width + offset:k * width + offset + channels] = v.astype(BF)


def clear_border(sh):
    blank = jnp.zeros((S, sh.shape[1]), sh.dtype)
    sh[0:S, :] = blank
    sh[sh.shape[0] - S:, :] = blank


def stage_first(x_ref, gain_ref, bias_ref, step_ref, rate_ref, tw_ref, o_ref, tv_ref, xt, *, size):
    cells, channels = o_ref.shape
    turn_in(x_ref, xt)
    mean, scale = norm_rows(xt, size, gain_ref[0:1, :])
    bias = bias_ref[0:1, :]

    def body(i, _):
        rows = pl.ds(pl.multiple_of(i * CHUNK, CHUNK), CHUNK)
        y = half_silu((xt[rows, :].astype(F32) - mean) * scale + bias)
        o_ref[rows, :] = y.astype(BF)
        return 0

    lax.fori_loop(0, cells // CHUNK, body, 0)
    angle = step_ref[0].astype(F32) * rate_ref[...]
    row = lax.broadcasted_iota(jnp.int32, angle.shape, 0)
    features = jnp.where(row < angle.shape[0] // 2, jnp.cos(angle), jnp.sin(angle))
    total = jnp.sum(tw_ref[...].astype(F32) * features, axis=0, keepdims=True)
    tv_ref[...] = total / (1.0 + jnp.exp(-total))


def stage_control(index_ref, x_ref, gain_ref, bias_ref, w_ref, far_ref, near_ref, xt, sh, *, size):
    cells = x_ref.shape[1]
    channels = x_ref.shape[0]
    j = pl.program_id(0)

    @pl.when(j == 0)
    def _():
        clear_border(sh)
        turn_in(x_ref, xt)
        mean, scale = norm_rows(xt, size, gain_ref[2:3, :])
        bias = bias_ref[2:3, :]
        left_ok, right_ok = edge_masks(CHUNK, channels)

        def body(i, _):
            start = pl.multiple_of(i * CHUNK, CHUNK)
            y = half_silu((xt[pl.ds(start, CHUNK), :].astype(F32) - mean) * scale + bias)
            store_shifted(sh, pl.multiple_of(start + S, S), y, left_ok, right_ok)
            return 0

        lax.fori_loop(0, cells // CHUNK, body, 0)

    lhs = jnp.concatenate([sh[S * dy:S * dy + cells, :] for dy in range(3)], axis=1)
    rhs = w_ref[...].reshape(w_ref.shape[0] * w_ref.shape[1], WIDE)
    product = jnp.dot(lhs, rhs, preferred_element_type=F32)
    for half in range(WIDE // LANES):
        value = product[:, half * LANES:(half + 1) * LANES]
        block = (2 * j + half) - index_ref[0] * (channels // LANES)
        inside = (block >= 0) & (block < channels // LANES)

        @pl.when(inside)
        def _():
            cols = pl.ds(pl.multiple_of(block * LANES, LANES), LANES)
            near_ref[:, cols] = value + xt[:, cols].astype(F32)

        @pl.when(jnp.logical_not(inside))
        def _():
            other = (2 * j + half) - (1 - index_ref[0]) * (channels // LANES)
            far_ref[:, pl.ds(pl.multiple_of(other * LANES, LANES), LANES)] = value.astype(BF)


def stage_hidden(index_ref, own_ref, got_ref, tv_ref, tvgot_ref, gain_ref, bias_ref, ut_ref, ct_ref, w_ref,
                 sh_ref, shift_ref, xs, acc, ushift, *, size):
    cells, channels = own_ref.shape
    s = pl.program_id(0)
    me = index_ref[0]
    mine = pl.ds(pl.multiple_of(me * channels, LANES), channels)
    theirs = pl.ds(pl.multiple_of((1 - me) * channels, LANES), channels)

    @pl.when(s == 0)
    def _():
        clear_border(xs)
        xs[S:S + cells, mine] = own_ref[...]
        xs[S:S + cells, theirs] = got_ref[...]

    def time_column(t_ref):
        a = jnp.sum(t_ref[:, mine].astype(F32) * tv_ref[...], axis=1, keepdims=True)
        return a + jnp.sum(t_ref[:, theirs].astype(F32) * tvgot_ref[...], axis=1, keepdims=True)

    @pl.when(s == 0)
    def _():
        ushift[...] = jnp.broadcast_to(time_column(ut_ref), ushift.shape)
        column = jnp.broadcast_to(time_column(ct_ref), (channels, LANES))
        for b in range(channels // LANES):
            part = slice(b * LANES, (b + 1) * LANES)
            shift_ref[:, part] = column[part, :].T[0:8, :]

    weights = jnp.concatenate([w_ref[k, 0] for k in range(3)], axis=1)
    col = lax.broadcasted_iota(jnp.int32, (8, WIDE), 1) % S
    for cb in range(cells // WIDE):
        rhs = jnp.concatenate([xs[S * dy + cb * WIDE:S * dy + cb * WIDE + WIDE, :] for dy in range(3)], axis=1)
        p = lax.dot_general(weights, rhs, (((1,), (1,)), ((), ())), preferred_element_type=F32)
        part = slice(cb * WIDE, (cb + 1) * WIDE)

        @pl.when(s == 0)
        def _():
            acc[:, part] = p

        @pl.when(s == 1)
        def _():
            moved = pltpu.roll(p, 1, 1).reshape(channels // 8, 8, WIDE)
            acc[:, part] += jnp.where((col != 0)[None], moved, 0.0).reshape(channels, WIDE)

        @pl.when(s == 2)
        def _():
            moved = pltpu.roll(p, WIDE - 1, 1).reshape(channels // 8, 8, WIDE)
            acc[:, part] += jnp.where((col != S - 1)[None], moved, 0.0).reshape(channels, WIDE)

    @pl.when(s == 2)
    def _():
        clear_border(sh_ref)
        count = 1.0 / (cells * size)

        def norm(g, _):
            rows = pl.ds(pl.multiple_of(g * size, 8), size)
            h = (acc[rows, :] + ushift[rows, 0:1]).astype(BF).astype(F32)
            mean = jnp.sum(jnp.sum(h, axis=0, keepdims=True), axis=1, keepdims=True) * count
            d = h - mean
            variance = jnp.sum(jnp.sum(d * d, axis=0, keepdims=True), axis=1, keepdims=True) * count
            scale = lax.rsqrt(variance + 1e-05) * gain_ref[rows, 1:2]
            acc[rows, :] = half_silu(d * scale + bias_ref[rows, 1:2])
            return 0

        lax.fori_loop(0, channels // size, norm, 0)
        left_ok, right_ok = edge_masks(WIDE, LANES)
        for b in range(channels // LANES):
            for cb in range(cells // WIDE):
                y = acc[b * LANES:(b + 1) * LANES, cb * WIDE:(cb + 1) * WIDE].T
                store_shifted(sh_ref, S + cb * WIDE, y, left_ok, right_ok, offset=b * LANES)


def gated_state(near_ref, got_ref, shift_ref, mask_ref, state):
    cells, channels = state.shape
    band = TILE * S
    where = lax.broadcasted_iota(jnp.int32, (band, channels), 0) % S // TILE

    def body(i, _):
        rows = pl.ds(pl.multiple_of(i * band, band), band)
        value = (near_ref[rows, :] + got_ref[rows, :].astype(F32) + shift_ref[0:1, :]).astype(BF).astype(F32)
        gate = jnp.zeros((band, channels), F32)
        for t in range(S // TILE):
            gate = jnp.where(where == t, mask_ref[i, t].astype(F32), gate)
        state[rows, :] = (value * gate).astype(BF)
        return 0

    lax.fori_loop(0, cells // band, body, 0)


def out_product(sh_ref, state, w_ref, z_ref):
    cells = state.shape[0]
    lhs = jnp.concatenate([sh_ref[S * dy:S * dy + cells, :] for dy in range(3)] + [state[...]], axis=1)
    rhs = jnp.concatenate([w_ref[...].reshape(w_ref.shape[0] * w_ref.shape[1], WIDE), z_ref[...]], axis=0)
    return jnp.dot(lhs, rhs, preferred_element_type=F32)


def stage_far(index_ref, mask_ref, sh_ref, near_ref, got_ref, shift_ref, w_ref, z_ref, far_ref, mixed_ref, state_ref):
    cells, channels = near_ref.shape
    j = pl.program_id(0)

    @pl.when(j == 0)
    def _():
        gated_state(near_ref, got_ref, shift_ref, mask_ref, state_ref)

    product = out_product(sh_ref, state_ref, w_ref, z_ref)
    for half in range(WIDE // LANES):
        value = product[:, half * LANES:(half + 1) * LANES]
        block = 2 * j + half - (1 - index_ref[0])
        inside = (block >= 0) & (block < channels // LANES)

        @pl.when(inside)
        def _():
            far_ref[:, pl.ds(pl.multiple_of(block * LANES, LANES), LANES)] = value.astype(BF)

        @pl.when(jnp.logical_not(inside))
        def _():
            mixed_ref[...] = value


def stage_near(index_ref, sh_ref, state_ref, w_ref, z_ref, o_ref):
    o_ref[...] = out_product(sh_ref, state_ref, w_ref, z_ref)


def stage_last(index_ref, x_ref, near_ref, mixed_ref, got_ref, o_ref):
    b = pl.program_id(0)
    is_mixed = b == jnp.where(index_ref[0] == 0, pl.num_programs(0) - 1, 0)
    local = jnp.where(is_mixed, mixed_ref[...], near_ref[...])
    total = local + got_ref[...].astype(F32)
    o_ref[...] = (x_ref[...].astype(F32) + total.T).astype(BF)


def whole(shape):
    return pl.BlockSpec(shape, lambda *_: (0,) * len(shape), pipeline_mode=pl.Buffered(1))


def params(mib):
    return pltpu.CompilerParams(vmem_limit_bytes=mib << 20)


def cost(flops, read):
    return pl.CostEstimate(flops=flops, bytes_accessed=read, transcendentals=0)


def local_pair(latent_x, control_h, tile_mask, timestep, time_weight, norm_gain, norm_bias, unet_conv_in,
               unet_conv_out, control_conv, unet_temb, control_temb, zero_conv):
    channels, cells = latent_x.shape
    full = unet_conv_in.shape[2]
    size = full // GROUPS
    swap = [(0, 1), (1, 0)]
    me = lax.axis_index("tensor").astype(jnp.int32).reshape(1)
    half_width = FREQ // 2
    rates = np.exp(-math.log(10000.0) * np.arange(half_width, dtype=np.float32) / half_width).astype(np.float32)
    rates = jnp.asarray(np.concatenate([rates, rates])[:, None])
    smem = pl.BlockSpec(memory_space=pltpu.SMEM)

    first, time_own = pl.pallas_call(
        functools.partial(stage_first, size=size),
        name="first",
        out_shape=(jax.ShapeDtypeStruct((cells, channels), BF), jax.ShapeDtypeStruct((1, channels), F32)),
        in_specs=[pl.BlockSpec(memory_space=pltpu.VMEM)] * 3 + [smem] + [pl.BlockSpec(memory_space=pltpu.VMEM)] * 2,
        out_specs=(pl.BlockSpec(memory_space=pltpu.VMEM),) * 2,
        scratch_shapes=[pltpu.VMEM((cells, channels), BF)],
        compiler_params=params(32),
        cost_estimate=cost(20 * cells * channels, 4 * cells * channels),
    )(latent_x, norm_gain, norm_bias, timestep, rates, time_weight)
    first_got = lax.ppermute(first, "tensor", swap)
    time_got = lax.ppermute(time_own, "tensor", swap)

    taps = control_conv.shape[0]
    conv_flops = 2 * taps * channels * full * cells
    conv_bytes = 2 * taps * channels * full
    control_far, control_near = pl.pallas_call(
        functools.partial(stage_control, size=size),
        name="control",
        out_shape=(jax.ShapeDtypeStruct((cells, channels), BF), jax.ShapeDtypeStruct((cells, channels), F32)),
        grid_spec=pltpu.PrefetchScalarGridSpec(
            num_scalar_prefetch=1,
            grid=(full // WIDE,),
            in_specs=[
                whole((channels, cells)),
                whole(norm_gain.shape),
                whole(norm_bias.shape),
                pl.BlockSpec((taps, channels, WIDE), lambda j, i: (0, 0, j)),
            ],
            out_specs=(whole((cells, channels)), whole((cells, channels))),
            scratch_shapes=[pltpu.VMEM((cells, channels), BF), pltpu.VMEM((cells + 2 * S, 3 * channels), BF)],
        ),
        compiler_params=params(40),
        cost_estimate=cost(conv_flops, conv_bytes),
    )(me, control_h, norm_gain, norm_bias, control_conv)
    control_got = lax.ppermute(control_far, "tensor", swap)

    columns = (norm_gain.T, norm_bias.T)
    shifted, control_shift = pl.pallas_call(
        functools.partial(stage_hidden, size=size),
        name="hidden",
        out_shape=(jax.ShapeDtypeStruct((cells + 2 * S, 3 * channels), BF), jax.ShapeDtypeStruct((8, channels), F32)),
        grid_spec=pltpu.PrefetchScalarGridSpec(
            num_scalar_prefetch=1,
            grid=(3,),
            in_specs=[
                whole((cells, channels)),
                whole((cells, channels)),
                whole((1, channels)),
                whole((1, channels)),
                whole(columns[0].shape),
                whole(columns[1].shape),
                whole(unet_temb.shape),
                whole(control_temb.shape),
                pl.BlockSpec((3, 1, channels, full), lambda s, i: (0, jnp.where(s == 0, 1, jnp.where(s == 1, 0, 2)), 0, 0)),
            ],
            out_specs=(whole((cells + 2 * S, 3 * channels)), whole((8, channels))),
            scratch_shapes=[
                pltpu.VMEM((cells + 2 * S, full), BF),
                pltpu.VMEM((channels, cells), F32),
                pltpu.VMEM((channels, LANES), F32),
            ],
        ),
        compiler_params=params(48),
        cost_estimate=cost(conv_flops, conv_bytes),
    )(me, first, first_got, time_own, time_got, *columns, unet_temb, control_temb,
      unet_conv_in.reshape(3, 3, channels, full))

    far_tiles = -(-channels // WIDE)
    near_tiles = full // WIDE - far_tiles
    mask = tile_mask.reshape(tile_mask.shape[1:])
    far, mixed, state = pl.pallas_call(
        stage_far,
        name="far",
        out_shape=(
            jax.ShapeDtypeStruct((cells, channels), BF),
            jax.ShapeDtypeStruct((cells, LANES), F32),
            jax.ShapeDtypeStruct((cells, channels), BF),
        ),
        grid_spec=pltpu.PrefetchScalarGridSpec(
            num_scalar_prefetch=1,
            grid=(far_tiles,),
            in_specs=[
                smem,
                whole((cells + 2 * S, 3 * channels)),
                whole((cells, channels)),
                whole((cells, channels)),
                whole((8, channels)),
                pl.BlockSpec((taps, channels, WIDE), lambda j, i: (0, 0, (1 - i[0]) * near_tiles + j)),
                pl.BlockSpec((channels, WIDE), lambda j, i: (0, (1 - i[0]) * near_tiles + j)),
            ],
            out_specs=(whole((cells, channels)), whole((cells, LANES)), whole((cells, channels))),
        ),
        compiler_params=params(40),
        cost_estimate=cost(conv_flops * far_tiles * WIDE // full, conv_bytes * far_tiles * WIDE // full),
    )(me, mask, shifted, control_near, control_got, control_shift, unet_conv_out, zero_conv)
    got = lax.ppermute(far, "tensor", swap)

    near = pl.pallas_call(
        stage_near,
        name="near",
        out_shape=jax.ShapeDtypeStruct((cells, near_tiles * WIDE), F32),
        grid_spec=pltpu.PrefetchScalarGridSpec(
            num_scalar_prefetch=1,
            grid=(near_tiles,),
            in_specs=[
                whole((cells + 2 * S, 3 * channels)),
                whole((cells, channels)),
                pl.BlockSpec((taps, channels, WIDE), lambda j, i: (0, 0, i[0] * far_tiles + j)),
                pl.BlockSpec((channels, WIDE), lambda j, i: (0, i[0] * far_tiles + j)),
            ],
            out_specs=pl.BlockSpec((cells, WIDE), lambda j, i: (0, j)),
        ),
        compiler_params=params(40),
        cost_estimate=cost(conv_flops * near_tiles * WIDE // full, conv_bytes * near_tiles * WIDE // full),
    )(me, shifted, state, unet_conv_out, zero_conv)

    last_near = near_tiles * WIDE // LANES - 1
    return pl.pallas_call(
        stage_last,
        name="last",
        out_shape=jax.ShapeDtypeStruct((channels, cells), BF),
        grid_spec=pltpu.PrefetchScalarGridSpec(
            num_scalar_prefetch=1,
            grid=(channels // LANES,),
            in_specs=[
                pl.BlockSpec((LANES, cells), lambda b, i: (b, 0)),
                pl.BlockSpec((cells, LANES), lambda b, i: (0, jnp.clip(b - i[0], 0, last_near))),
                whole((cells, LANES)),
                pl.BlockSpec((cells, LANES), lambda b, i: (0, b)),
            ],
            out_specs=pl.BlockSpec((LANES, cells), lambda b, i: (b, 0)),
        ),
        compiler_params=params(24),
        cost_estimate=cost(4 * channels * cells, 10 * channels * cells),
    )(me, latent_x, near, mixed, got)


def norm_silu(inputs, scales, shifts):
    rows_count = inputs.shape[0]
    group_size = C // GROUPS
    grouped = inputs.astype(jnp.float32).reshape(rows_count // group_size, group_size, VIEWS, S * S)
    average = jnp.mean(grouped, axis=(1, 3), keepdims=True)
    centred = grouped - average
    variance = jnp.mean(centred * centred, axis=(1, 3), keepdims=True)
    normed = (centred * lax.rsqrt(variance + 1e-05)).reshape(rows_count, VIEWS * S * S)
    return jax.nn.silu(normed * scales[:, None] + shifts[:, None]).astype(jnp.bfloat16)


def tap_mask(place, cells):
    where = jnp.arange(cells, dtype=jnp.int32)
    row_index = where // S % S + (place // 3 - 1)
    col_index = where % S + (place % 3 - 1)
    inside = (row_index >= 0) & (row_index < S) & (col_index >= 0) & (col_index < S)
    return inside.astype(jnp.float32)


def shift_cells(values, place):
    cells = values.shape[1]
    offset_cells = (place // 3 - 1) * S + (place % 3 - 1)
    padded = jnp.pad(values, ((0, 0), (S + 1, S + 1)))
    moved = lax.slice_in_dim(padded, S + 1 + offset_cells, S + 1 + offset_cells + cells, axis=1)
    return moved * tap_mask(place, cells)[None, :]


def conv_plain(weights, inputs, running):
    for place in range(9):
        product = jnp.dot(weights[place], inputs, preferred_element_type=jnp.float32)
        running = running + shift_cells(product, place)
    return running


def conv_flipped(weights, inputs):
    running = None
    for place in range(9):
        product = lax.dot_general(
            weights[place], inputs, (((0,), (0,)), ((), ())), preferred_element_type=jnp.float32
        )
        moved = shift_cells(product, place)
        running = moved if running is None else running + moved
    return running


def expand_mask(tile_mask):
    blocks = tile_mask.astype(jnp.float32)[:, :, None, :, None]
    spread_mask = jnp.broadcast_to(blocks, (VIEWS, S // TILE, TILE, S // TILE, TILE))
    return spread_mask.reshape(VIEWS * S * S)


def local_any(
    latent_x,
    control_h,
    tile_mask,
    timestep,
    time_weight,
    norm_gain,
    norm_bias,
    unet_conv_in,
    unet_conv_out,
    control_conv,
    unet_temb,
    control_temb,
    zero_conv,
):
    local_time = jax.nn.silu(
        jnp.dot(
            timestep_features(timestep),
            time_weight.astype(jnp.float32),
            precision=lax.Precision.HIGHEST,
        )
    )
    time_vector = lax.all_gather(local_time, "tensor", axis=0, tiled=True)
    unet_shift = jnp.dot(
        unet_temb.astype(jnp.float32), time_vector, precision=lax.Precision.HIGHEST
    )
    control_shift = jnp.dot(
        control_temb.astype(jnp.float32), time_vector, precision=lax.Precision.HIGHEST
    )
    gate_row = expand_mask(tile_mask)
    channels = latent_x.shape[0]
    first = norm_silu(latent_x, norm_gain[0], norm_bias[0])
    initial = jnp.zeros((channels, latent_x.shape[1]), jnp.float32)
    weights = unet_conv_in
    hidden_sum = conv_plain(weights, lax.all_gather(first, "tensor", axis=0, tiled=True), initial)
    hidden = (hidden_sum + unet_shift[:, None]).astype(jnp.bfloat16)
    hidden = lax.optimization_barrier(hidden)
    second = norm_silu(hidden, norm_gain[1], norm_bias[1])
    control_act = norm_silu(control_h, norm_gain[2], norm_bias[2])
    weights = control_conv
    control_sum = lax.psum_scatter(
        conv_flipped(weights, control_act).astype(jnp.bfloat16),
        "tensor",
        scatter_dimension=0,
        tiled=True,
    ).astype(jnp.float32)
    control_state = (control_h.astype(jnp.float32) + control_sum + control_shift[:, None]).astype(
        jnp.bfloat16
    )
    weights = zero_conv
    product = lax.dot_general(
        weights, control_state, (((0,), (0,)), ((), ())), preferred_element_type=jnp.float32
    )
    weights = unet_conv_out
    combined = lax.psum_scatter(
        (conv_flipped(weights, second) + product * gate_row[None, :]).astype(jnp.bfloat16),
        "tensor",
        scatter_dimension=0,
        tiled=True,
    ).astype(jnp.float32)
    return (latent_x.astype(jnp.float32) + combined).astype(jnp.bfloat16)


def solution(mesh):
    placed = (
        P("tensor", "dp"),
        P("tensor", "dp"),
        P("dp", None, None),
        P("dp"),
        P(None, "tensor"),
        P(None, "tensor"),
        P(None, "tensor"),
        P(None, "tensor", None),
        P(None, "tensor", None),
        P(None, "tensor", None),
        P("tensor", None),
        P("tensor", None),
        P("tensor", None),
    )

    def local(latent_x, *rest):
        channels, cells = latent_x.shape
        paired = mesh.shape["tensor"] == 2 and channels % WIDE == LANES and VIEWS == 1 and cells == S * S
        return (local_pair if paired else local_any)(latent_x, *rest)

    return jax.shard_map(
        local, mesh=mesh, in_specs=placed, out_specs=P("tensor", "dp"), check_vma=False
    )
```

```python
import functools
import math

import jax
import jax.numpy as jnp
import numpy as np
from jax import lax
from jax.experimental import pallas as pl
from jax.experimental.pallas import tpu as pltpu
from jax.sharding import PartitionSpec as P

C = 1280
GROUPS = 32
FREQ = 320
S = 32
TILE = 4
VIEWS = 1

BF = jnp.bfloat16
F32 = jnp.float32
WIDE = 256
LANES = 128
CHUNK = 2 * S
FRONT_MIB = 32
COVER_MIB = 24
MIDDLE_MIB = 52
LAST_MIB = 16


def timestep_features(timestep):
    half_width = FREQ // 2
    rates = jnp.exp(-math.log(10000.0) * jnp.arange(half_width, dtype=jnp.float32) / half_width)
    angles = timestep.astype(jnp.float32)[0] * rates
    return jnp.concatenate([jnp.cos(angles), jnp.sin(angles)])


NT = (((1,), (1,)), ((), ()))


def half_silu(v):
    h = 0.5 * v
    return h + h * jnp.tanh(h)


def group_masks(channels, size):
    groups = channels // size
    row = lax.broadcasted_iota(jnp.int32, (groups, channels), 0)
    col = lax.broadcasted_iota(jnp.int32, (groups, channels), 1)
    return ((col >= row * size) & (col < row * size + size)).astype(F32)


def group_mean(sums, mask, count):
    per_group = jnp.sum(mask * sums, axis=1, keepdims=True) * (1.0 / count)
    return jnp.sum(mask * per_group, axis=0, keepdims=True)


def each_chunk(cells, body, carry):
    return lax.fori_loop(0, cells // CHUNK, lambda i, c: body(pl.multiple_of(i * CHUNK, CHUNK), c), carry)


def norm_rows(xt, size, gain):
    cells, channels = xt.shape
    mask = group_masks(channels, size)

    def fold(value):
        return jnp.sum(value.reshape(CHUNK // 8, 8, channels), axis=0)

    def add(start, total):
        return total + fold(xt[pl.ds(start, CHUNK), :].astype(F32))

    total = each_chunk(cells, add, jnp.zeros((8, channels), F32))
    mean = group_mean(jnp.sum(total, axis=0, keepdims=True), mask, cells * size)

    def add_square(start, total):
        d = xt[pl.ds(start, CHUNK), :].astype(F32) - mean
        return total + fold(d * d)

    total = each_chunk(cells, add_square, jnp.zeros((8, channels), F32))
    variance = group_mean(jnp.sum(total, axis=0, keepdims=True), mask, cells * size)
    return mean, lax.rsqrt(variance + 1e-05) * gain


def turn_in(x_ref, xt):
    channels = x_ref.shape[0]
    for b in range(channels // LANES):
        part = slice(b * LANES, (b + 1) * LANES)
        xt[:, part] = x_ref[part, :].T


def edge_masks(rows, channels):
    col = lax.broadcasted_iota(jnp.int32, (rows, channels), 0) % S
    return col != 0, col != S - 1


def activate(xt, sh, mean, scale, bias):
    cells, channels = xt.shape
    left_ok, right_ok = edge_masks(CHUNK, channels)

    def body(start, _):
        y = half_silu((xt[pl.ds(start, CHUNK), :].astype(F32) - mean) * scale + bias)
        lo = jnp.where(left_ok, pltpu.roll(y, 1, 0), 0.0)
        hi = jnp.where(right_ok, pltpu.roll(y, CHUNK - 1, 0), 0.0)
        for k, v in enumerate((lo, y, hi)):
            sh[pl.ds(start + S, CHUNK), k * channels:(k + 1) * channels] = v.astype(BF)
        return 0

    each_chunk(cells, body, 0)


def clear_border(sh):
    blank = jnp.zeros((S, sh.shape[1]), sh.dtype)
    sh[0:S, :] = blank
    sh[sh.shape[0] - S:, :] = blank


def split3(row):
    hi = row.astype(BF)
    rest = row - hi.astype(F32)
    mid = rest.astype(BF)
    low = (rest - mid.astype(F32)).astype(BF)
    place = lax.broadcasted_iota(jnp.int32, (8, row.shape[1]), 0)
    parts = jnp.where(place == 0, hi.astype(F32), jnp.where(place == 1, mid.astype(F32), low.astype(F32)))
    return jnp.where(place < 3, parts, 0.0).astype(BF)


def conv_tile(sh, w, extra=None, z=None):
    cells = sh.shape[0] - 2 * S
    lhs = [sh[S * dy:S * dy + cells, :] for dy in range(3)]
    rhs = w.reshape(w.shape[0] * w.shape[1], w.shape[2])
    if extra is not None:
        lhs.append(extra)
        rhs = jnp.concatenate([rhs, z], axis=0)
    return jnp.dot(jnp.concatenate(lhs, axis=1), rhs, preferred_element_type=F32)


def keep_far(j, tiles, product, me, far, mixed):
    far[:, columns_of(j)] = product.astype(BF)

    @pl.when((j == 0) & (me == 0))
    def _():
        mixed[...] = product[:, :LANES]

    @pl.when((j == tiles - 1) & (me == 1))
    def _():
        mixed[...] = product[:, LANES:]


def columns_of(tile):
    return pl.ds(pl.multiple_of(tile * WIDE, WIDE), WIDE)


def far_columns(me, channels):
    return pl.ds(pl.multiple_of((1 - me) * LANES, LANES), channels)


def stage_front(me_ref, step_ref, x_hbm, h_hbm, gain_hbm, bias_hbm, rate_hbm, tw_hbm, w_hbm,
                first_hbm, tv_hbm, far_hbm, mixed_hbm, ht_hbm, sh,
                xv, hv, xt, ht, gain, bias, rate, tw, w, first, tv, far, mixed, sems, *, size, tiles):
    channels, cells = hv.shape
    me = me_ref[0]
    far_tiles = -(-channels // WIDE)
    start_tile = (1 - me) * (tiles - far_tiles)

    def bring(src, dst, k):
        c = pltpu.make_async_copy(src, dst, sems.at[k])
        c.start()
        return c

    def weights(j):
        return pltpu.make_async_copy(w_hbm.at[:, :, columns_of(start_tile + j)], w.at[j], sems.at[8 + j])

    c_h = bring(h_hbm, hv, 0)
    c_g = bring(gain_hbm, gain, 1)
    c_b = bring(bias_hbm, bias, 2)
    c_x = bring(x_hbm, xv, 3)
    c_r = bring(rate_hbm, rate, 4)
    c_t = bring(tw_hbm, tw, 5)
    for j in range(far_tiles):
        weights(j).start()
    clear_border(sh)
    c_h.wait()
    turn_in(hv, ht)
    out_ht = bring(ht, ht_hbm, 6)
    c_g.wait()
    c_b.wait()
    mean, scale = norm_rows(ht, size, gain[2:3, :])
    activate(ht, sh, mean, scale, bias[2:3, :])
    c_x.wait()
    c_r.wait()
    c_t.wait()

    turn_in(xv, xt)
    mean, scale = norm_rows(xt, size, gain[0:1, :])
    shift = bias[0:1, :]

    def body(start, _):
        y = half_silu((xt[pl.ds(start, CHUNK), :].astype(F32) - mean) * scale + shift)
        first[pl.ds(start, CHUNK), :] = y.astype(BF)
        return 0

    each_chunk(cells, body, 0)
    out_first = bring(first, first_hbm, 0)
    angle = step_ref[0].astype(F32) * rate[...]
    row = lax.broadcasted_iota(jnp.int32, angle.shape, 0)
    features = jnp.where(row < angle.shape[0] // 2, jnp.cos(angle), jnp.sin(angle))
    total = jnp.sum(tw[...].astype(F32) * features, axis=0, keepdims=True)
    tv[...] = total / (1.0 + jnp.exp(-total))
    out_tv = bring(tv, tv_hbm, 7)

    def tile(j, _):
        weights(j).wait()
        keep_far(j, far_tiles, conv_tile(sh, w[j]), me, far, mixed)
        return 0

    lax.fori_loop(0, far_tiles, tile, 0)
    out_far = bring(far.at[:, far_columns(me, channels)], far_hbm, 1)
    out_mixed = bring(mixed, mixed_hbm, 2)
    for c in (out_ht, out_tv, out_first, out_far, out_mixed):
        c.wait()


def stage_cover(me_ref, sh, w_hbm, near_hbm, w, near, sems, *, tiles):
    channels = w_hbm.shape[1]
    me = me_ref[0]
    far_tiles = -(-channels // WIDE)
    near_tiles = tiles - far_tiles

    def weights(j):
        return pltpu.make_async_copy(w_hbm.at[:, :, columns_of(me * far_tiles + j)], w.at[j], sems.at[j])

    def result(j):
        return pltpu.make_async_copy(
            near.at[:, columns_of(j)], near_hbm.at[:, columns_of(j)], sems.at[near_tiles + j])

    for j in range(near_tiles):
        weights(j).start()

    def tile(j, _):
        weights(j).wait()
        near[:, columns_of(j)] = conv_tile(sh, w[j])
        result(j).start()
        return 0

    lax.fori_loop(0, near_tiles, tile, 0)
    for j in range(near_tiles):
        result(j).wait()


def stage_middle(me_ref, mask_ref, own_hbm, got_hbm, tv_hbm, tvgot_hbm, gain_hbm, bias_hbm, ut_hbm, ct_hbm, win_hbm,
                 wout_hbm, z_hbm, near_hbm, mixed_hbm, ht_hbm, cgot_hbm,
                 far_hbm, mix_hbm, sh, state,
                 xs, acc, xt, tv, tvgot, gain, bias, ut, ct, win, wout, z, near, ht, cgot, far, mix, sems,
                 *, size, tiles):
    cells, channels = xt.shape
    full = xs.shape[1]
    me = me_ref[0]
    far_tiles = -(-channels // WIDE)
    near_wide = near_hbm.shape[1]
    start_tile = (1 - me) * (tiles - far_tiles)
    mine = pl.ds(pl.multiple_of(me * channels, LANES), channels)
    theirs = pl.ds(pl.multiple_of((1 - me) * channels, LANES), channels)
    places = (1, 0, 2)

    count = [0]

    def bring(src, dst):
        c = pltpu.make_async_copy(src, dst, sems.at[count[0]])
        count[0] += 1
        c.start()
        return c

    c_x = [bring(own_hbm, xs.at[pl.ds(S, cells), mine]), bring(got_hbm, xs.at[pl.ds(S, cells), theirs])]
    c_in = [bring(win_hbm.at[:, places[0]], win.at[0])]
    small = [bring(a, b) for a, b in ((tv_hbm, tv), (tvgot_hbm, tvgot), (gain_hbm, gain), (bias_hbm, bias),
                                      (ut_hbm, ut), (ct_hbm, ct))]
    clear_border(xs)
    clear_border(sh)
    c_in.append(bring(win_hbm.at[:, places[1]], win.at[1]))
    side = [
        bring(near_hbm, near.at[:, pl.ds(pl.multiple_of(me * LANES, LANES), near_wide)]),
        bring(mixed_hbm, near.at[:, pl.ds(pl.multiple_of((1 - me) * near_wide, LANES), LANES)]),
        bring(ht_hbm, ht),
        bring(cgot_hbm, cgot),
    ]
    base = 17

    def out_weights(j):
        at = columns_of(start_tile + j)
        return (
            pltpu.make_async_copy(wout_hbm.at[:, :, at], wout.at[j], sems.at[base + 2 * j]),
            pltpu.make_async_copy(z_hbm.at[:, at], z.at[j], sems.at[base + 2 * j + 1]),
        )

    for j in range(far_tiles):
        for c in out_weights(j):
            c.start()
    for c in c_x + small:
        c.wait()

    def time_row(t_ref):
        a = lax.dot_general(split3(tv[...]), t_ref[:, mine], NT, preferred_element_type=F32)
        a = a + lax.dot_general(split3(tvgot[...]), t_ref[:, theirs], NT, preferred_element_type=F32)
        return jnp.sum(a, axis=0, keepdims=True)

    band = TILE * S
    where = lax.broadcasted_iota(jnp.int32, (band, LANES), 0) % S // TILE

    def gated_band(i, control_shift):
        rows = slice(i * band, (i + 1) * band)
        gate = jnp.zeros((band, LANES), F32)
        for t in range(S // TILE):
            gate = jnp.where(where == t, mask_ref[i, t].astype(F32), gate)
        for b in range(channels // LANES):
            part = slice(b * LANES, (b + 1) * LANES)
            value = near[rows, part] + cgot[rows, part].astype(F32) + ht[rows, part].astype(F32)
            value = (value + control_shift[:, part]).astype(BF).astype(F32)
            state[rows, part] = (value * gate).astype(BF)

    bands = cells // band
    blocks = cells // WIDE
    col = lax.broadcasted_iota(jnp.int32, (channels, WIDE), 1) % S
    for s, place in enumerate(places):
        c_in[s].wait()
        if s == 1:
            for c in side:
                c.wait()
            control_shift = time_row(ct)
        weights = jnp.concatenate([win[s % 2, k] for k in range(3)], axis=1)
        for cb in range(blocks):
            rhs = jnp.concatenate([xs[S * dy + cb * WIDE:S * dy + cb * WIDE + WIDE, :] for dy in range(3)], axis=1)
            p = lax.dot_general(weights, rhs, NT, preferred_element_type=F32)
            part = slice(cb * WIDE, (cb + 1) * WIDE)
            if place == 1:
                acc[:, part] = p
            elif place == 0:
                acc[:, part] += jnp.where(col != 0, pltpu.roll(p, 1, 1), 0.0)
            else:
                acc[:, part] += jnp.where(col != S - 1, pltpu.roll(p, WIDE - 1, 1), 0.0)
            if s == 1:
                for i in range(cb * bands // blocks, (cb + 1) * bands // blocks):
                    gated_band(i, control_shift)
        if s == 0:
            c_in.append(bring(win_hbm.at[:, places[2]], win.at[0]))

    unet_shift = time_row(ut)
    for b in range(channels // LANES):
        part = slice(b * LANES, (b + 1) * LANES)
        xt[:, part] = (acc[part, :].T + unet_shift[:, part]).astype(BF)
    mean, scale = norm_rows(xt, size, gain[1:2, :])
    activate(xt, sh, mean, scale, bias[1:2, :])

    def tile(j, _):
        for c in out_weights(j):
            c.wait()
        keep_far(j, far_tiles, conv_tile(sh, wout[j], state[...], z[j]), me, far, mix)
        return 0

    lax.fori_loop(0, far_tiles, tile, 0)
    last = [bring(far.at[:, far_columns(me, channels)], far_hbm), bring(mix, mix_hbm)]
    for c in last:
        c.wait()


def stage_near(me_ref, sh, state, w_hbm, z_hbm, near_hbm, w, z, near, sems, *, tiles):
    channels = w_hbm.shape[1]
    me = me_ref[0]
    far_tiles = -(-channels // WIDE)
    near_tiles = tiles - far_tiles

    def weights(j):
        at = columns_of(me * far_tiles + j)
        return (
            pltpu.make_async_copy(w_hbm.at[:, :, at], w.at[j], sems.at[2 * j]),
            pltpu.make_async_copy(z_hbm.at[:, at], z.at[j], sems.at[2 * j + 1]),
        )

    def result(j):
        return pltpu.make_async_copy(
            near.at[:, columns_of(j)], near_hbm.at[:, columns_of(j)], sems.at[2 * near_tiles + j])

    for j in range(near_tiles):
        for c in weights(j):
            c.start()

    def tile(j, _):
        for c in weights(j):
            c.wait()
        near[:, columns_of(j)] = conv_tile(sh, w[j], state[...], z[j])
        result(j).start()
        return 0

    lax.fori_loop(0, near_tiles, tile, 0)
    for j in range(near_tiles):
        result(j).wait()


def stage_last(me_ref, x_ref, near_ref, mixed_ref, got_ref, o_ref):
    b = pl.program_id(0)
    is_mixed = b == jnp.where(me_ref[0] == 0, pl.num_programs(0) - 1, 0)
    local = jnp.where(is_mixed, mixed_ref[...], near_ref[...])
    total = local + got_ref[...].astype(F32)
    o_ref[...] = (x_ref[...].astype(F32) + total.T).astype(BF)


def whole(shape):
    return pl.BlockSpec(shape, lambda *_: (0,) * len(shape), pipeline_mode=pl.Buffered(1))


def params(mib):
    return pltpu.CompilerParams(vmem_limit_bytes=mib << 20)


def far_off(*arrays):
    return [pltpu.with_memory_space_constraint(a, pltpu.HBM) for a in arrays]


def close(*arrays):
    return [pltpu.with_memory_space_constraint(a, pltpu.VMEM) for a in arrays]


def cost(flops, read):
    return pl.CostEstimate(flops=flops, bytes_accessed=read, transcendentals=0)


def local_pair(latent_x, control_h, tile_mask, timestep, time_weight, norm_gain, norm_bias, unet_conv_in,
               unet_conv_out, control_conv, unet_temb, control_temb, zero_conv):
    channels, cells = latent_x.shape
    full = unet_conv_in.shape[2]
    size = full // GROUPS
    swap = [(0, 1), (1, 0)]
    me = lax.axis_index("tensor").astype(jnp.int32).reshape(1)
    half_width = FREQ // 2
    rates = np.exp(-math.log(10000.0) * np.arange(half_width, dtype=np.float32) / half_width).astype(np.float32)
    rates = jnp.asarray(np.concatenate([rates, rates])[:, None])
    smem = pl.BlockSpec(memory_space=pltpu.SMEM)
    anywhere = pl.BlockSpec(memory_space=pl.ANY)
    vmem = pl.BlockSpec(memory_space=pltpu.VMEM)
    dma = pltpu.SemaphoreType.DMA
    tiles = full // WIDE
    far_tiles = -(-channels // WIDE)
    near_tiles = tiles - far_tiles
    taps = control_conv.shape[0]
    act = pltpu.HBM((cells, channels), BF)
    padded = pltpu.VMEM((cells + 2 * S, 3 * channels), BF)
    half_tile = pltpu.HBM((cells, LANES), F32)
    near_out = pltpu.HBM((cells, near_tiles * WIDE), F32)
    conv_flops = 2 * taps * channels * full * cells
    conv_bytes = 2 * taps * channels * full

    first, time_own, control_far, control_mixed, control_t, shifted = pl.pallas_call(
        functools.partial(stage_front, size=size, tiles=tiles),
        name="front",
        out_shape=(act, pltpu.HBM((1, channels), F32), act, half_tile, act, padded),
        in_specs=[smem, smem] + [anywhere] * 7,
        out_specs=(anywhere,) * 5 + (vmem,),
        scratch_shapes=[
            pltpu.VMEM((channels, cells), BF),
            pltpu.VMEM((channels, cells), BF),
            pltpu.VMEM((cells, channels), BF),
            pltpu.VMEM((cells, channels), BF),
            pltpu.VMEM(norm_gain.shape, F32),
            pltpu.VMEM(norm_bias.shape, F32),
            pltpu.VMEM(rates.shape, F32),
            pltpu.VMEM(time_weight.shape, BF),
            pltpu.VMEM((far_tiles, taps, channels, WIDE), BF),
            pltpu.VMEM((cells, channels), BF),
            pltpu.VMEM((1, channels), F32),
            pltpu.VMEM((cells, far_tiles * WIDE), BF),
            pltpu.VMEM((cells, LANES), F32),
            dma((8 + far_tiles,)),
        ],
        compiler_params=params(FRONT_MIB),
        cost_estimate=cost(conv_flops * far_tiles // tiles, conv_bytes * far_tiles // tiles),
    )(me, timestep, *far_off(latent_x, control_h, norm_gain, norm_bias, rates, time_weight, control_conv))
    first_got = lax.ppermute(first, "tensor", swap)
    time_got = lax.ppermute(time_own, "tensor", swap)
    control_got = lax.ppermute(control_far, "tensor", swap)

    control_near = pl.pallas_call(
        functools.partial(stage_cover, tiles=tiles),
        name="cover",
        out_shape=near_out,
        in_specs=[smem, vmem, anywhere],
        out_specs=anywhere,
        scratch_shapes=[
            pltpu.VMEM((near_tiles, taps, channels, WIDE), BF),
            pltpu.VMEM(near_out.shape, F32),
            dma((2 * near_tiles,)),
        ],
        compiler_params=params(COVER_MIB),
        cost_estimate=cost(conv_flops * near_tiles // tiles, conv_bytes * near_tiles // tiles),
    )(me, *close(shifted), *far_off(control_conv))

    mask = tile_mask.reshape(tile_mask.shape[1:])
    far, mixed, second, state = pl.pallas_call(
        functools.partial(stage_middle, size=size, tiles=tiles),
        name="middle",
        out_shape=(act, half_tile, padded, pltpu.VMEM((cells, channels), BF)),
        in_specs=[smem, smem] + [anywhere] * 15,
        out_specs=(anywhere, anywhere, vmem, vmem),
        scratch_shapes=[
            pltpu.VMEM((cells + 2 * S, full), BF),
            pltpu.VMEM((channels, cells), F32),
            pltpu.VMEM((cells, channels), BF),
            pltpu.VMEM((1, channels), F32),
            pltpu.VMEM((1, channels), F32),
            pltpu.VMEM(norm_gain.shape, F32),
            pltpu.VMEM(norm_bias.shape, F32),
            pltpu.VMEM(unet_temb.shape, BF),
            pltpu.VMEM(control_temb.shape, BF),
            pltpu.VMEM((2, 3, channels, full), BF),
            pltpu.VMEM((far_tiles, taps, channels, WIDE), BF),
            pltpu.VMEM((far_tiles, channels, WIDE), BF),
            pltpu.VMEM((cells, channels), F32),
            pltpu.VMEM((cells, channels), BF),
            pltpu.VMEM((cells, channels), BF),
            pltpu.VMEM((cells, far_tiles * WIDE), BF),
            pltpu.VMEM((cells, LANES), F32),
            dma((17 + 2 * far_tiles,)),
        ],
        compiler_params=params(MIDDLE_MIB),
        cost_estimate=cost(conv_flops * (tiles + far_tiles) // tiles, conv_bytes * (tiles + far_tiles) // tiles),
    )(me, mask, *far_off(first, first_got, time_own, time_got, norm_gain, norm_bias, unet_temb, control_temb,
                         unet_conv_in.reshape(3, 3, channels, full), unet_conv_out, zero_conv, control_near,
                         control_mixed, control_t, control_got))
    got = lax.ppermute(far, "tensor", swap)

    near = pl.pallas_call(
        functools.partial(stage_near, tiles=tiles),
        name="near",
        out_shape=near_out,
        in_specs=[smem, vmem, vmem, anywhere, anywhere],
        out_specs=anywhere,
        scratch_shapes=[
            pltpu.VMEM((near_tiles, taps, channels, WIDE), BF),
            pltpu.VMEM((near_tiles, channels, WIDE), BF),
            pltpu.VMEM(near_out.shape, F32),
            dma((3 * near_tiles,)),
        ],
        compiler_params=params(COVER_MIB),
        cost_estimate=cost(conv_flops * near_tiles // tiles, conv_bytes * near_tiles // tiles),
    )(me, *close(second, state), *far_off(unet_conv_out, zero_conv))

    last_near = near_tiles * WIDE // LANES - 1
    return pl.pallas_call(
        stage_last,
        name="last",
        out_shape=jax.ShapeDtypeStruct((channels, cells), BF),
        grid_spec=pltpu.PrefetchScalarGridSpec(
            num_scalar_prefetch=1,
            grid=(channels // LANES,),
            in_specs=[
                pl.BlockSpec((LANES, cells), lambda b, i: (b, 0)),
                pl.BlockSpec((cells, LANES), lambda b, i: (0, jnp.clip(b - i[0], 0, last_near))),
                whole((cells, LANES)),
                pl.BlockSpec((cells, LANES), lambda b, i: (0, b)),
            ],
            out_specs=pl.BlockSpec((LANES, cells), lambda b, i: (b, 0)),
        ),
        compiler_params=params(LAST_MIB),
        cost_estimate=cost(4 * channels * cells, 10 * channels * cells),
    )(me, latent_x, near, mixed, got)


def norm_silu(inputs, scales, shifts):
    rows_count = inputs.shape[0]
    group_size = C // GROUPS
    grouped = inputs.astype(jnp.float32).reshape(rows_count // group_size, group_size, VIEWS, S * S)
    average = jnp.mean(grouped, axis=(1, 3), keepdims=True)
    centred = grouped - average
    variance = jnp.mean(centred * centred, axis=(1, 3), keepdims=True)
    normed = (centred * lax.rsqrt(variance + 1e-05)).reshape(rows_count, VIEWS * S * S)
    return jax.nn.silu(normed * scales[:, None] + shifts[:, None]).astype(jnp.bfloat16)


def tap_mask(place, cells):
    where = jnp.arange(cells, dtype=jnp.int32)
    row_index = where // S % S + (place // 3 - 1)
    col_index = where % S + (place % 3 - 1)
    inside = (row_index >= 0) & (row_index < S) & (col_index >= 0) & (col_index < S)
    return inside.astype(jnp.float32)


def shift_cells(values, place):
    cells = values.shape[1]
    offset_cells = (place // 3 - 1) * S + (place % 3 - 1)
    padded = jnp.pad(values, ((0, 0), (S + 1, S + 1)))
    moved = lax.slice_in_dim(padded, S + 1 + offset_cells, S + 1 + offset_cells + cells, axis=1)
    return moved * tap_mask(place, cells)[None, :]


def conv_plain(weights, inputs, running):
    for place in range(9):
        product = jnp.dot(weights[place], inputs, preferred_element_type=jnp.float32)
        running = running + shift_cells(product, place)
    return running


def conv_flipped(weights, inputs):
    running = None
    for place in range(9):
        product = lax.dot_general(
            weights[place], inputs, (((0,), (0,)), ((), ())), preferred_element_type=jnp.float32
        )
        moved = shift_cells(product, place)
        running = moved if running is None else running + moved
    return running


def expand_mask(tile_mask):
    blocks = tile_mask.astype(jnp.float32)[:, :, None, :, None]
    spread_mask = jnp.broadcast_to(blocks, (VIEWS, S // TILE, TILE, S // TILE, TILE))
    return spread_mask.reshape(VIEWS * S * S)


def local_any(
    latent_x,
    control_h,
    tile_mask,
    timestep,
    time_weight,
    norm_gain,
    norm_bias,
    unet_conv_in,
    unet_conv_out,
    control_conv,
    unet_temb,
    control_temb,
    zero_conv,
):
    local_time = jax.nn.silu(
        jnp.dot(
            timestep_features(timestep),
            time_weight.astype(jnp.float32),
            precision=lax.Precision.HIGHEST,
        )
    )
    time_vector = lax.all_gather(local_time, "tensor", axis=0, tiled=True)
    unet_shift = jnp.dot(
        unet_temb.astype(jnp.float32), time_vector, precision=lax.Precision.HIGHEST
    )
    control_shift = jnp.dot(
        control_temb.astype(jnp.float32), time_vector, precision=lax.Precision.HIGHEST
    )
    gate_row = expand_mask(tile_mask)
    channels = latent_x.shape[0]
    first = norm_silu(latent_x, norm_gain[0], norm_bias[0])
    initial = jnp.zeros((channels, latent_x.shape[1]), jnp.float32)
    weights = unet_conv_in
    hidden_sum = conv_plain(weights, lax.all_gather(first, "tensor", axis=0, tiled=True), initial)
    hidden = (hidden_sum + unet_shift[:, None]).astype(jnp.bfloat16)
    hidden = lax.optimization_barrier(hidden)
    second = norm_silu(hidden, norm_gain[1], norm_bias[1])
    control_act = norm_silu(control_h, norm_gain[2], norm_bias[2])
    weights = control_conv
    control_sum = lax.psum_scatter(
        conv_flipped(weights, control_act).astype(jnp.bfloat16),
        "tensor",
        scatter_dimension=0,
        tiled=True,
    ).astype(jnp.float32)
    control_state = (control_h.astype(jnp.float32) + control_sum + control_shift[:, None]).astype(
        jnp.bfloat16
    )
    weights = zero_conv
    product = lax.dot_general(
        weights, control_state, (((0,), (0,)), ((), ())), preferred_element_type=jnp.float32
    )
    weights = unet_conv_out
    combined = lax.psum_scatter(
        (conv_flipped(weights, second) + product * gate_row[None, :]).astype(jnp.bfloat16),
        "tensor",
        scatter_dimension=0,
        tiled=True,
    ).astype(jnp.float32)
    return (latent_x.astype(jnp.float32) + combined).astype(jnp.bfloat16)


def solution(mesh):
    placed = (
        P("tensor", "dp"),
        P("tensor", "dp"),
        P("dp", None, None),
        P("dp"),
        P(None, "tensor"),
        P(None, "tensor"),
        P(None, "tensor"),
        P(None, "tensor", None),
        P(None, "tensor", None),
        P(None, "tensor", None),
        P("tensor", None),
        P("tensor", None),
        P("tensor", None),
    )

    def local(latent_x, *rest):
        channels, cells = latent_x.shape
        paired = mesh.shape["tensor"] == 2 and channels % WIDE == LANES and VIEWS == 1 and cells == S * S
        return (local_pair if paired else local_any)(latent_x, *rest)

    return jax.shard_map(
        local, mesh=mesh, in_specs=placed, out_specs=P("tensor", "dp"), check_vma=False
    )
```

```python
import functools
import math

import jax
import jax.numpy as jnp
import numpy as np
from jax import lax
from jax.experimental import pallas as pl
from jax.experimental.pallas import tpu as pltpu
from jax.sharding import PartitionSpec as P

C = 1280
GROUPS = 32
FREQ = 320
S = 32
TILE = 4
VIEWS = 1

BF = jnp.bfloat16
F32 = jnp.float32
WIDE = 256
LANES = 128
CHUNK = 2 * S
NORM = 8 * S
FRONT_MIB = 32
COVER_MIB = 24
MIDDLE_MIB = 48
LAST_MIB = 16


def timestep_features(timestep):
    half_width = FREQ // 2
    rates = jnp.exp(-math.log(10000.0) * jnp.arange(half_width, dtype=jnp.float32) / half_width)
    angles = timestep.astype(jnp.float32)[0] * rates
    return jnp.concatenate([jnp.cos(angles), jnp.sin(angles)])


NT = (((1,), (1,)), ((), ()))


def silu_of_half(h):
    return h + h * jnp.tanh(h)


def group_masks(channels, size):
    groups = channels // size
    row = lax.broadcasted_iota(jnp.int32, (groups, channels), 0)
    col = lax.broadcasted_iota(jnp.int32, (groups, channels), 1)
    return ((col >= row * size) & (col < row * size + size)).astype(F32)


def group_mean(sums, mask, count):
    per_group = jnp.sum(mask * sums, axis=1, keepdims=True) * (1.0 / count)
    return jnp.sum(mask * per_group, axis=0, keepdims=True)


def each_chunk(cells, body, carry, rows=CHUNK):
    return lax.fori_loop(0, cells // rows, lambda i, c: body(pl.multiple_of(i * rows, rows), c), carry)


def norm_rows(xt, size, gain):
    cells, channels = xt.shape
    mask = group_masks(channels, size)

    def fold(value):
        return jnp.sum(value.reshape(NORM // 8, 8, channels), axis=0)

    def add(start, total):
        return total + fold(xt[pl.ds(start, NORM), :].astype(F32))

    total = each_chunk(cells, add, jnp.zeros((8, channels), F32), NORM)
    mean = group_mean(jnp.sum(total, axis=0, keepdims=True), mask, cells * size)

    def add_square(start, total):
        d = xt[pl.ds(start, NORM), :].astype(F32) - mean
        return total + fold(d * d)

    total = each_chunk(cells, add_square, jnp.zeros((8, channels), F32), NORM)
    variance = group_mean(jnp.sum(total, axis=0, keepdims=True), mask, cells * size)
    return mean, lax.rsqrt(variance + 1e-05) * (0.5 * gain)


def turn_in(x_ref, xt):
    channels = x_ref.shape[0]
    for b in range(channels // LANES):
        part = slice(b * LANES, (b + 1) * LANES)
        xt[:, part] = x_ref[part, :].T


def edge_masks(rows, channels):
    col = lax.broadcasted_iota(jnp.int32, (rows, channels), 0) % S
    return col != 0, col != S - 1


def activate(xt, sh, mean, scale, bias):
    cells, channels = xt.shape
    bias = 0.5 * bias
    left_ok, right_ok = edge_masks(CHUNK, channels)

    def body(start, _):
        y = silu_of_half((xt[pl.ds(start, CHUNK), :].astype(F32) - mean) * scale + bias)
        lo = jnp.where(left_ok, pltpu.roll(y, 1, 0), 0.0)
        hi = jnp.where(right_ok, pltpu.roll(y, CHUNK - 1, 0), 0.0)
        for k, v in enumerate((lo, y, hi)):
            sh[pl.ds(start + S, CHUNK), k * channels:(k + 1) * channels] = v.astype(BF)
        return 0

    each_chunk(cells, body, 0)


def clear_border(sh):
    blank = jnp.zeros((S, sh.shape[1]), sh.dtype)
    sh[0:S, :] = blank
    sh[sh.shape[0] - S:, :] = blank


def split3(row):
    hi = row.astype(BF)
    rest = row - hi.astype(F32)
    mid = rest.astype(BF)
    low = (rest - mid.astype(F32)).astype(BF)
    place = lax.broadcasted_iota(jnp.int32, (8, row.shape[1]), 0)
    parts = jnp.where(place == 0, hi.astype(F32), jnp.where(place == 1, mid.astype(F32), low.astype(F32)))
    return jnp.where(place < 3, parts, 0.0).astype(BF)


def conv_tile(sh, w, extra=None, z=None):
    cells = sh.shape[0] - 2 * S
    lhs = [sh[S * dy:S * dy + cells, :] for dy in range(3)]
    rhs = w.reshape(w.shape[0] * w.shape[1], w.shape[2])
    if extra is not None:
        lhs.append(extra)
        rhs = jnp.concatenate([rhs, z], axis=0)
    return jnp.dot(jnp.concatenate(lhs, axis=1), rhs, preferred_element_type=F32)


def keep_far(j, tiles, product, me, far, mixed):
    far[:, columns_of(j)] = product.astype(BF)

    @pl.when((j == 0) & (me == 0))
    def _():
        mixed[...] = product[:, :LANES]

    @pl.when((j == tiles - 1) & (me == 1))
    def _():
        mixed[...] = product[:, LANES:]


def columns_of(tile):
    return pl.ds(pl.multiple_of(tile * WIDE, WIDE), WIDE)


def far_columns(me, channels):
    return pl.ds(pl.multiple_of((1 - me) * LANES, LANES), channels)


def stage_front(me_ref, step_ref, x_hbm, h_hbm, gain_hbm, bias_hbm, rate_hbm, tw_hbm, w_hbm,
                first_hbm, tv_hbm, far_hbm, mixed_hbm, ht_hbm, sh,
                xv, hv, xt, ht, gain, bias, rate, tw, w, first, tv, far, mixed, sems, *, size, tiles):
    channels, cells = hv.shape
    me = me_ref[0]
    far_tiles = -(-channels // WIDE)
    start_tile = (1 - me) * (tiles - far_tiles)

    def bring(src, dst, k):
        c = pltpu.make_async_copy(src, dst, sems.at[k])
        c.start()
        return c

    def weights(j):
        return pltpu.make_async_copy(w_hbm.at[:, :, columns_of(start_tile + j)], w.at[j], sems.at[8 + j])

    c_h = bring(h_hbm, hv, 0)
    c_g = bring(gain_hbm, gain, 1)
    c_b = bring(bias_hbm, bias, 2)
    clear_border(sh)
    c_h.wait()
    c_x = bring(x_hbm, xv, 3)
    c_r = bring(rate_hbm, rate, 4)
    c_t = bring(tw_hbm, tw, 5)
    for j in range(far_tiles):
        weights(j).start()
    turn_in(hv, ht)
    out_ht = bring(ht, ht_hbm, 6)
    c_g.wait()
    c_b.wait()
    mean, scale = norm_rows(ht, size, gain[2:3, :])
    activate(ht, sh, mean, scale, bias[2:3, :])
    c_x.wait()
    c_r.wait()
    c_t.wait()

    turn_in(xv, xt)
    mean, scale = norm_rows(xt, size, gain[0:1, :])
    shift = 0.5 * bias[0:1, :]

    def body(start, _):
        y = silu_of_half((xt[pl.ds(start, CHUNK), :].astype(F32) - mean) * scale + shift)
        first[pl.ds(start, CHUNK), :] = y.astype(BF)
        return 0

    each_chunk(cells, body, 0)
    out_first = bring(first, first_hbm, 0)
    angle = step_ref[0].astype(F32) * rate[...]
    col = lax.broadcasted_iota(jnp.int32, angle.shape, 1)
    features = jnp.where(col < angle.shape[1] // 2, jnp.cos(angle), jnp.sin(angle))
    total = jnp.sum(jnp.dot(split3(features), tw[...], preferred_element_type=F32), axis=0, keepdims=True)
    tv[...] = total / (1.0 + jnp.exp(-total))
    out_tv = bring(tv, tv_hbm, 7)

    def tile(j, _):
        weights(j).wait()
        keep_far(j, far_tiles, conv_tile(sh, w[j]), me, far, mixed)
        return 0

    lax.fori_loop(0, far_tiles, tile, 0)
    out_far = bring(far.at[:, far_columns(me, channels)], far_hbm, 1)
    out_mixed = bring(mixed, mixed_hbm, 2)
    for c in (out_ht, out_tv, out_first, out_far, out_mixed):
        c.wait()


def stage_cover(me_ref, sh, w_hbm, near_hbm, w, near, sems, *, tiles):
    channels = w_hbm.shape[1]
    me = me_ref[0]
    far_tiles = -(-channels // WIDE)
    near_tiles = tiles - far_tiles

    def weights(j):
        return pltpu.make_async_copy(w_hbm.at[:, :, columns_of(me * far_tiles + j)], w.at[j], sems.at[j])

    def result(j):
        return pltpu.make_async_copy(
            near.at[:, columns_of(j)], near_hbm.at[:, columns_of(j)], sems.at[near_tiles + j])

    weights(0).start()

    def tile(j, _):
        weights(j).wait()

        @pl.when(j + 1 < near_tiles)
        def _():
            weights(j + 1).start()

        near[:, columns_of(j)] = conv_tile(sh, w[j])
        result(j).start()
        return 0

    lax.fori_loop(0, near_tiles, tile, 0)
    for j in range(near_tiles):
        result(j).wait()


def stage_middle(me_ref, mask_ref, got_ref, tvgot, cgot, own_hbm, tv_hbm, gain_hbm, bias_hbm, ut_hbm, ct_hbm, win_hbm,
                 wout_hbm, z_hbm, near_hbm, mixed_hbm, ht_hbm,
                 far_hbm, mix_hbm, sh, state,
                 xs, acc, xt, tv, gain, bias, ut, ct, win, wout, z, near, ht, far, mix, sems,
                 *, size, tiles):
    cells, channels = xt.shape
    full = xs.shape[1]
    me = me_ref[0]
    far_tiles = -(-channels // WIDE)
    near_wide = near_hbm.shape[1]
    start_tile = (1 - me) * (tiles - far_tiles)
    mine = pl.ds(pl.multiple_of(me * channels, LANES), channels)
    theirs = pl.ds(pl.multiple_of((1 - me) * channels, LANES), channels)
    places = (1, 0, 2)

    count = [0]

    def bring(src, dst):
        c = pltpu.make_async_copy(src, dst, sems.at[count[0]])
        count[0] += 1
        c.start()
        return c

    c_x = [bring(own_hbm, xs.at[pl.ds(S, cells), mine])]
    c_in = [bring(win_hbm.at[:, places[0]], win.at[0])]
    clear_border(xs)
    clear_border(sh)
    xs[S:S + cells, theirs] = got_ref[...]
    base = 17

    def out_weights(j):
        at = columns_of(start_tile + j)
        return (
            pltpu.make_async_copy(wout_hbm.at[:, :, at], wout.at[j], sems.at[base + 2 * j]),
            pltpu.make_async_copy(z_hbm.at[:, at], z.at[j], sems.at[base + 2 * j + 1]),
        )

    c_x[0].wait()
    c_in[0].wait()
    small = [bring(a, b) for a, b in ((tv_hbm, tv), (gain_hbm, gain), (bias_hbm, bias), (ut_hbm, ut), (ct_hbm, ct))]
    side = [
        bring(near_hbm, near.at[:, pl.ds(pl.multiple_of(me * LANES, LANES), near_wide)]),
        bring(mixed_hbm, near.at[:, pl.ds(pl.multiple_of((1 - me) * near_wide, LANES), LANES)]),
        bring(ht_hbm, ht),
    ]
    c_in.append(bring(win_hbm.at[:, places[1]], win.at[1]))

    def time_row(t_ref):
        a = lax.dot_general(split3(tv[...]), t_ref[:, mine], NT, preferred_element_type=F32)
        a = a + lax.dot_general(split3(tvgot[...]), t_ref[:, theirs], NT, preferred_element_type=F32)
        return jnp.sum(a, axis=0, keepdims=True)

    band = TILE * S
    where = lax.broadcasted_iota(jnp.int32, (band, LANES), 0) % S // TILE

    def gated_band(i, control_shift):
        rows = slice(i * band, (i + 1) * band)
        gate = jnp.zeros((band, LANES), F32)
        for t in range(S // TILE):
            gate = jnp.where(where == t, mask_ref[i, t].astype(F32), gate)
        for b in range(channels // LANES):
            part = slice(b * LANES, (b + 1) * LANES)
            value = near[rows, part] + cgot[rows, part].astype(F32) + ht[rows, part].astype(F32)
            state[rows, part] = ((value + control_shift[:, part]) * gate).astype(BF)

    bands = cells // band
    blocks = cells // WIDE
    col = lax.broadcasted_iota(jnp.int32, (channels, WIDE), 1) % S
    for s, place in enumerate(places):
        if s > 0:
            c_in[s].wait()
        if s == 1:
            for c in small + side:
                c.wait()
            control_shift = time_row(ct)
        weights = jnp.concatenate([win[s % 2, k] for k in range(3)], axis=1)
        for cb in range(blocks):
            rhs = jnp.concatenate([xs[S * dy + cb * WIDE:S * dy + cb * WIDE + WIDE, :] for dy in range(3)], axis=1)
            p = lax.dot_general(weights, rhs, NT, preferred_element_type=F32)
            part = slice(cb * WIDE, (cb + 1) * WIDE)
            if place == 1:
                acc[:, part] = p
            elif place == 0:
                acc[:, part] += jnp.where(col != 0, pltpu.roll(p, 1, 1), 0.0)
            else:
                acc[:, part] += jnp.where(col != S - 1, pltpu.roll(p, WIDE - 1, 1), 0.0)
            if s == 1:
                for i in range(cb * bands // blocks, (cb + 1) * bands // blocks):
                    gated_band(i, control_shift)
        if s == 0:
            c_in.append(bring(win_hbm.at[:, places[2]], win.at[0]))
            for j in range(far_tiles):
                for c in out_weights(j):
                    c.start()

    unet_shift = time_row(ut)
    for b in range(channels // LANES):
        part = slice(b * LANES, (b + 1) * LANES)
        xt[:, part] = (acc[part, :].T + unet_shift[:, part]).astype(BF)
    mean, scale = norm_rows(xt, size, gain[1:2, :])
    activate(xt, sh, mean, scale, bias[1:2, :])

    def tile(j, _):
        for c in out_weights(j):
            c.wait()
        keep_far(j, far_tiles, conv_tile(sh, wout[j], state[...], z[j]), me, far, mix)
        return 0

    lax.fori_loop(0, far_tiles, tile, 0)
    last = [bring(far.at[:, far_columns(me, channels)], far_hbm), bring(mix, mix_hbm)]
    for c in last:
        c.wait()


def stage_near(me_ref, sh, state, w_hbm, z_hbm, near, w, z, sems, *, tiles):
    channels = w_hbm.shape[1]
    me = me_ref[0]
    far_tiles = -(-channels // WIDE)
    near_tiles = tiles - far_tiles

    def weights(j):
        at = columns_of(me * far_tiles + j)
        return (
            pltpu.make_async_copy(w_hbm.at[:, :, at], w.at[j], sems.at[2 * j]),
            pltpu.make_async_copy(z_hbm.at[:, at], z.at[j], sems.at[2 * j + 1]),
        )

    for c in weights(0):
        c.start()

    def tile(j, _):
        for c in weights(j):
            c.wait()

        @pl.when(j + 1 < near_tiles)
        def _():
            for c in weights(j + 1):
                c.start()

        near[:, columns_of(j)] = conv_tile(sh, w[j], state[...], z[j])
        return 0

    lax.fori_loop(0, near_tiles, tile, 0)


def stage_last(me_ref, x_ref, near_ref, mixed_ref, got_ref, o_ref):
    b = pl.program_id(0)
    is_mixed = b == jnp.where(me_ref[0] == 0, pl.num_programs(0) - 1, 0)
    local = jnp.where(is_mixed, mixed_ref[...], near_ref[...])
    total = local + got_ref[...].astype(F32)
    o_ref[...] = (x_ref[...].astype(F32) + total.T).astype(BF)


def whole(shape):
    return pl.BlockSpec(shape, lambda *_: (0,) * len(shape), pipeline_mode=pl.Buffered(1))


def params(mib):
    return pltpu.CompilerParams(vmem_limit_bytes=mib << 20)


def far_off(*arrays):
    return [pltpu.with_memory_space_constraint(a, pltpu.HBM) for a in arrays]


def close(*arrays):
    return [pltpu.with_memory_space_constraint(a, pltpu.VMEM) for a in arrays]


def cost(flops, read):
    return pl.CostEstimate(flops=flops, bytes_accessed=read, transcendentals=0)


def local_pair(latent_x, control_h, tile_mask, timestep, time_weight, norm_gain, norm_bias, unet_conv_in,
               unet_conv_out, control_conv, unet_temb, control_temb, zero_conv):
    channels, cells = latent_x.shape
    full = unet_conv_in.shape[2]
    size = full // GROUPS
    swap = [(0, 1), (1, 0)]
    me = lax.axis_index("tensor").astype(jnp.int32).reshape(1)
    half_width = FREQ // 2
    rates = np.exp(-math.log(10000.0) * np.arange(half_width, dtype=np.float32) / half_width).astype(np.float32)
    rates = jnp.asarray(np.concatenate([rates, rates])[None, :])
    smem = pl.BlockSpec(memory_space=pltpu.SMEM)
    anywhere = pl.BlockSpec(memory_space=pl.ANY)
    vmem = pl.BlockSpec(memory_space=pltpu.VMEM)
    dma = pltpu.SemaphoreType.DMA
    tiles = full // WIDE
    far_tiles = -(-channels // WIDE)
    near_tiles = tiles - far_tiles
    taps = control_conv.shape[0]
    act = pltpu.HBM((cells, channels), BF)
    padded = pltpu.VMEM((cells + 2 * S, 3 * channels), BF)
    half_tile = pltpu.HBM((cells, LANES), F32)
    near_out = pltpu.HBM((cells, near_tiles * WIDE), F32)
    conv_flops = 2 * taps * channels * full * cells
    conv_bytes = 2 * taps * channels * full

    first, time_own, control_far, control_mixed, control_t, shifted = pl.pallas_call(
        functools.partial(stage_front, size=size, tiles=tiles),
        name="front",
        out_shape=(act, pltpu.HBM((1, channels), F32), act, half_tile, act, padded),
        in_specs=[smem, smem] + [anywhere] * 7,
        out_specs=(anywhere,) * 5 + (vmem,),
        scratch_shapes=[
            pltpu.VMEM((channels, cells), BF),
            pltpu.VMEM((channels, cells), BF),
            pltpu.VMEM((cells, channels), BF),
            pltpu.VMEM((cells, channels), BF),
            pltpu.VMEM(norm_gain.shape, F32),
            pltpu.VMEM(norm_bias.shape, F32),
            pltpu.VMEM(rates.shape, F32),
            pltpu.VMEM(time_weight.shape, BF),
            pltpu.VMEM((far_tiles, taps, channels, WIDE), BF),
            pltpu.VMEM((cells, channels), BF),
            pltpu.VMEM((1, channels), F32),
            pltpu.VMEM((cells, far_tiles * WIDE), BF),
            pltpu.VMEM((cells, LANES), F32),
            dma((8 + far_tiles,)),
        ],
        compiler_params=params(FRONT_MIB),
        cost_estimate=cost(conv_flops * far_tiles // tiles, conv_bytes * far_tiles // tiles),
    )(me, timestep, *far_off(latent_x, control_h, norm_gain, norm_bias, rates, time_weight, control_conv))
    first_got = lax.ppermute(first, "tensor", swap)
    time_got = lax.ppermute(time_own, "tensor", swap)
    control_got = lax.ppermute(control_far, "tensor", swap)

    control_near = pl.pallas_call(
        functools.partial(stage_cover, tiles=tiles),
        name="cover",
        out_shape=near_out,
        in_specs=[smem, vmem, anywhere],
        out_specs=anywhere,
        scratch_shapes=[
            pltpu.VMEM((near_tiles, taps, channels, WIDE), BF),
            pltpu.VMEM(near_out.shape, F32),
            dma((2 * near_tiles,)),
        ],
        compiler_params=params(COVER_MIB),
        cost_estimate=cost(conv_flops * near_tiles // tiles, conv_bytes * near_tiles // tiles),
    )(me, *close(shifted), *far_off(control_conv))

    mask = tile_mask.reshape(tile_mask.shape[1:])
    far, mixed, second, state = pl.pallas_call(
        functools.partial(stage_middle, size=size, tiles=tiles),
        name="middle",
        out_shape=(act, half_tile, padded, pltpu.VMEM((cells, channels), BF)),
        in_specs=[smem, smem, vmem, vmem, vmem] + [anywhere] * 12,
        out_specs=(anywhere, anywhere, vmem, vmem),
        scratch_shapes=[
            pltpu.VMEM((cells + 2 * S, full), BF),
            pltpu.VMEM((channels, cells), F32),
            pltpu.VMEM((cells, channels), BF),
            pltpu.VMEM((1, channels), F32),
            pltpu.VMEM(norm_gain.shape, F32),
            pltpu.VMEM(norm_bias.shape, F32),
            pltpu.VMEM(unet_temb.shape, BF),
            pltpu.VMEM(control_temb.shape, BF),
            pltpu.VMEM((2, 3, channels, full), BF),
            pltpu.VMEM((far_tiles, taps, channels, WIDE), BF),
            pltpu.VMEM((far_tiles, channels, WIDE), BF),
            pltpu.VMEM((cells, channels), F32),
            pltpu.VMEM((cells, channels), BF),
            pltpu.VMEM((cells, far_tiles * WIDE), BF),
            pltpu.VMEM((cells, LANES), F32),
            dma((17 + 2 * far_tiles,)),
        ],
        compiler_params=params(MIDDLE_MIB),
        cost_estimate=cost(conv_flops * (tiles + far_tiles) // tiles, conv_bytes * (tiles + far_tiles) // tiles),
    )(me, mask, *close(first_got, time_got, control_got),
      *far_off(first, time_own, norm_gain, norm_bias, unet_temb, control_temb,
               unet_conv_in.reshape(3, 3, channels, full), unet_conv_out, zero_conv, control_near,
               control_mixed, control_t))
    got = lax.ppermute(far, "tensor", swap)

    near = pl.pallas_call(
        functools.partial(stage_near, tiles=tiles),
        name="near",
        out_shape=pltpu.VMEM(near_out.shape, F32),
        in_specs=[smem, vmem, vmem, anywhere, anywhere],
        out_specs=vmem,
        scratch_shapes=[
            pltpu.VMEM((near_tiles, taps, channels, WIDE), BF),
            pltpu.VMEM((near_tiles, channels, WIDE), BF),
            dma((2 * near_tiles,)),
        ],
        compiler_params=params(COVER_MIB),
        cost_estimate=cost(conv_flops * near_tiles // tiles, conv_bytes * near_tiles // tiles),
    )(me, *close(second, state), *far_off(unet_conv_out, zero_conv))

    last_near = near_tiles * WIDE // LANES - 1
    return pl.pallas_call(
        stage_last,
        name="last",
        out_shape=jax.ShapeDtypeStruct((channels, cells), BF),
        grid_spec=pltpu.PrefetchScalarGridSpec(
            num_scalar_prefetch=1,
            grid=(channels // LANES,),
            in_specs=[
                pl.BlockSpec((LANES, cells), lambda b, i: (b, 0)),
                pl.BlockSpec((cells, LANES), lambda b, i: (0, jnp.clip(b - i[0], 0, last_near))),
                whole((cells, LANES)),
                pl.BlockSpec((cells, LANES), lambda b, i: (0, b)),
            ],
            out_specs=pl.BlockSpec((LANES, cells), lambda b, i: (b, 0)),
        ),
        compiler_params=params(LAST_MIB),
        cost_estimate=cost(4 * channels * cells, 10 * channels * cells),
    )(me, latent_x, near, mixed, got)


def norm_silu(inputs, scales, shifts):
    rows_count = inputs.shape[0]
    group_size = C // GROUPS
    grouped = inputs.astype(jnp.float32).reshape(rows_count // group_size, group_size, VIEWS, S * S)
    average = jnp.mean(grouped, axis=(1, 3), keepdims=True)
    centred = grouped - average
    variance = jnp.mean(centred * centred, axis=(1, 3), keepdims=True)
    normed = (centred * lax.rsqrt(variance + 1e-05)).reshape(rows_count, VIEWS * S * S)
    return jax.nn.silu(normed * scales[:, None] + shifts[:, None]).astype(jnp.bfloat16)


def tap_mask(place, cells):
    where = jnp.arange(cells, dtype=jnp.int32)
    row_index = where // S % S + (place // 3 - 1)
    col_index = where % S + (place % 3 - 1)
    inside = (row_index >= 0) & (row_index < S) & (col_index >= 0) & (col_index < S)
    return inside.astype(jnp.float32)


def shift_cells(values, place):
    cells = values.shape[1]
    offset_cells = (place // 3 - 1) * S + (place % 3 - 1)
    padded = jnp.pad(values, ((0, 0), (S + 1, S + 1)))
    moved = lax.slice_in_dim(padded, S + 1 + offset_cells, S + 1 + offset_cells + cells, axis=1)
    return moved * tap_mask(place, cells)[None, :]


def conv_plain(weights, inputs, running):
    for place in range(9):
        product = jnp.dot(weights[place], inputs, preferred_element_type=jnp.float32)
        running = running + shift_cells(product, place)
    return running


def conv_flipped(weights, inputs):
    running = None
    for place in range(9):
        product = lax.dot_general(
            weights[place], inputs, (((0,), (0,)), ((), ())), preferred_element_type=jnp.float32
        )
        moved = shift_cells(product, place)
        running = moved if running is None else running + moved
    return running


def expand_mask(tile_mask):
    blocks = tile_mask.astype(jnp.float32)[:, :, None, :, None]
    spread_mask = jnp.broadcast_to(blocks, (VIEWS, S // TILE, TILE, S // TILE, TILE))
    return spread_mask.reshape(VIEWS * S * S)


def local_any(
    latent_x,
    control_h,
    tile_mask,
    timestep,
    time_weight,
    norm_gain,
    norm_bias,
    unet_conv_in,
    unet_conv_out,
    control_conv,
    unet_temb,
    control_temb,
    zero_conv,
):
    local_time = jax.nn.silu(
        jnp.dot(
            timestep_features(timestep),
            time_weight.astype(jnp.float32),
            precision=lax.Precision.HIGHEST,
        )
    )
    time_vector = lax.all_gather(local_time, "tensor", axis=0, tiled=True)
    unet_shift = jnp.dot(
        unet_temb.astype(jnp.float32), time_vector, precision=lax.Precision.HIGHEST
    )
    control_shift = jnp.dot(
        control_temb.astype(jnp.float32), time_vector, precision=lax.Precision.HIGHEST
    )
    gate_row = expand_mask(tile_mask)
    channels = latent_x.shape[0]
    first = norm_silu(latent_x, norm_gain[0], norm_bias[0])
    initial = jnp.zeros((channels, latent_x.shape[1]), jnp.float32)
    weights = unet_conv_in
    hidden_sum = conv_plain(weights, lax.all_gather(first, "tensor", axis=0, tiled=True), initial)
    hidden = (hidden_sum + unet_shift[:, None]).astype(jnp.bfloat16)
    hidden = lax.optimization_barrier(hidden)
    second = norm_silu(hidden, norm_gain[1], norm_bias[1])
    control_act = norm_silu(control_h, norm_gain[2], norm_bias[2])
    weights = control_conv
    control_sum = lax.psum_scatter(
        conv_flipped(weights, control_act).astype(jnp.bfloat16),
        "tensor",
        scatter_dimension=0,
        tiled=True,
    ).astype(jnp.float32)
    control_state = (control_h.astype(jnp.float32) + control_sum + control_shift[:, None]).astype(
        jnp.bfloat16
    )
    weights = zero_conv
    product = lax.dot_general(
        weights, control_state, (((0,), (0,)), ((), ())), preferred_element_type=jnp.float32
    )
    weights = unet_conv_out
    combined = lax.psum_scatter(
        (conv_flipped(weights, second) + product * gate_row[None, :]).astype(jnp.bfloat16),
        "tensor",
        scatter_dimension=0,
        tiled=True,
    ).astype(jnp.float32)
    return (latent_x.astype(jnp.float32) + combined).astype(jnp.bfloat16)


def solution(mesh):
    placed = (
        P("tensor", "dp"),
        P("tensor", "dp"),
        P("dp", None, None),
        P("dp"),
        P(None, "tensor"),
        P(None, "tensor"),
        P(None, "tensor"),
        P(None, "tensor", None),
        P(None, "tensor", None),
        P(None, "tensor", None),
        P("tensor", None),
        P("tensor", None),
        P("tensor", None),
    )

    def local(latent_x, *rest):
        channels, cells = latent_x.shape
        paired = mesh.shape["tensor"] == 2 and channels % WIDE == LANES and VIEWS == 1 and cells == S * S
        return (local_pair if paired else local_any)(latent_x, *rest)

    return jax.shard_map(
        local, mesh=mesh, in_specs=placed, out_specs=P("tensor", "dp"), check_vma=False
    )
```

```python
import functools
import math

import jax
import jax.numpy as jnp
import numpy as np
from jax import lax
from jax.experimental import pallas as pl
from jax.experimental.pallas import tpu as pltpu
from jax.sharding import PartitionSpec as P

C = 1280
GROUPS = 32
FREQ = 320
S = 32
TILE = 4
VIEWS = 1

BF = jnp.bfloat16
F32 = jnp.float32
WIDE = 256
LANES = 128
CHUNK = 4 * S
NORM = 8 * S
FRONT_MIB = 32
COVER_MIB = 24
MIDDLE_MIB = 48
LAST_MIB = 16


def timestep_features(timestep):
    half_width = FREQ // 2
    rates = jnp.exp(-math.log(10000.0) * jnp.arange(half_width, dtype=jnp.float32) / half_width)
    angles = timestep.astype(jnp.float32)[0] * rates
    return jnp.concatenate([jnp.cos(angles), jnp.sin(angles)])


NT = (((1,), (1,)), ((), ()))


def silu_of_half(h):
    return h + h * jnp.tanh(h)


def group_masks(channels, size):
    groups = channels // size
    row = lax.broadcasted_iota(jnp.int32, (groups, channels), 0)
    col = lax.broadcasted_iota(jnp.int32, (groups, channels), 1)
    return ((col >= row * size) & (col < row * size + size)).astype(F32)


def group_mean(sums, mask, count):
    per_group = jnp.sum(mask * sums, axis=1, keepdims=True) * (1.0 / count)
    return jnp.sum(mask * per_group, axis=0, keepdims=True)


def each_chunk(cells, body, carry, rows=CHUNK):
    return lax.fori_loop(0, cells // rows, lambda i, c: body(pl.multiple_of(i * rows, rows), c), carry)


def norm_rows(xt, size, gain):
    cells, channels = xt.shape
    mask = group_masks(channels, size)

    def fold(value):
        return jnp.sum(value.reshape(NORM // 8, 8, channels), axis=0)

    def add(start, total):
        return total + fold(xt[pl.ds(start, NORM), :].astype(F32))

    total = each_chunk(cells, add, jnp.zeros((8, channels), F32), NORM)
    mean = group_mean(jnp.sum(total, axis=0, keepdims=True), mask, cells * size)

    def add_square(start, total):
        d = xt[pl.ds(start, NORM), :].astype(F32) - mean
        return total + fold(d * d)

    total = each_chunk(cells, add_square, jnp.zeros((8, channels), F32), NORM)
    variance = group_mean(jnp.sum(total, axis=0, keepdims=True), mask, cells * size)
    return mean, lax.rsqrt(variance + 1e-05) * (0.5 * gain)


def turn_in(x_ref, xt):
    channels = x_ref.shape[0]
    for b in range(channels // LANES):
        part = slice(b * LANES, (b + 1) * LANES)
        xt[:, part] = x_ref[part, :].T


def edge_masks(rows, channels):
    col = lax.broadcasted_iota(jnp.int32, (rows, channels), 0) % S
    return col != 0, col != S - 1


def activate(xt, sh, mean, scale, bias):
    cells, channels = xt.shape
    bias = 0.5 * bias
    left_ok, right_ok = edge_masks(CHUNK, channels)

    def body(start, _):
        y = silu_of_half((xt[pl.ds(start, CHUNK), :].astype(F32) - mean) * scale + bias)
        lo = jnp.where(left_ok, pltpu.roll(y, 1, 0), 0.0)
        hi = jnp.where(right_ok, pltpu.roll(y, CHUNK - 1, 0), 0.0)
        for k, v in enumerate((lo, y, hi)):
            sh[pl.ds(start + S, CHUNK), k * channels:(k + 1) * channels] = v.astype(BF)
        return 0

    each_chunk(cells, body, 0)


def clear_border(sh):
    blank = jnp.zeros((S, sh.shape[1]), sh.dtype)
    sh[0:S, :] = blank
    sh[sh.shape[0] - S:, :] = blank


def split3(row):
    hi = row.astype(BF)
    rest = row - hi.astype(F32)
    mid = rest.astype(BF)
    low = (rest - mid.astype(F32)).astype(BF)
    place = lax.broadcasted_iota(jnp.int32, (8, row.shape[1]), 0)
    parts = jnp.where(place == 0, hi.astype(F32), jnp.where(place == 1, mid.astype(F32), low.astype(F32)))
    return jnp.where(place < 3, parts, 0.0).astype(BF)


def conv_tile(sh, w, extra=None, z=None):
    cells = sh.shape[0] - 2 * S
    lhs = [sh[S * dy:S * dy + cells, :] for dy in range(3)]
    rhs = w.reshape(w.shape[0] * w.shape[1], w.shape[2])
    if extra is not None:
        lhs.append(extra)
        rhs = jnp.concatenate([rhs, z], axis=0)
    return jnp.dot(jnp.concatenate(lhs, axis=1), rhs, preferred_element_type=F32)


def keep_far(j, tiles, product, me, far, mixed):
    far[:, columns_of(j)] = product.astype(BF)

    @pl.when((j == 0) & (me == 0))
    def _():
        mixed[...] = product[:, :LANES]

    @pl.when((j == tiles - 1) & (me == 1))
    def _():
        mixed[...] = product[:, LANES:]


def columns_of(tile):
    return pl.ds(pl.multiple_of(tile * WIDE, WIDE), WIDE)


def far_columns(me, channels):
    return pl.ds(pl.multiple_of((1 - me) * LANES, LANES), channels)


def stage_front(me_ref, step_ref, x_hbm, h_hbm, gain_hbm, bias_hbm, rate_hbm, tw_hbm, w_hbm,
                first_hbm, tv_hbm, far_hbm, mixed_hbm, ht_hbm, sh,
                xv, hv, xt, ht, gain, bias, rate, tw, w, first, tv, far, mixed, sems, *, size, tiles):
    channels, cells = hv.shape
    me = me_ref[0]
    far_tiles = -(-channels // WIDE)
    start_tile = (1 - me) * (tiles - far_tiles)

    def bring(src, dst, k):
        c = pltpu.make_async_copy(src, dst, sems.at[k])
        c.start()
        return c

    def weights(j):
        return pltpu.make_async_copy(w_hbm.at[:, :, columns_of(start_tile + j)], w.at[j], sems.at[8 + j])

    c_h = bring(h_hbm, hv, 0)
    c_g = bring(gain_hbm, gain, 1)
    c_b = bring(bias_hbm, bias, 2)
    clear_border(sh)
    c_h.wait()
    c_x = bring(x_hbm, xv, 3)
    c_r = bring(rate_hbm, rate, 4)
    c_t = bring(tw_hbm, tw, 5)
    for j in range(far_tiles):
        weights(j).start()
    turn_in(hv, ht)
    out_ht = bring(ht, ht_hbm, 6)
    c_g.wait()
    c_b.wait()
    mean, scale = norm_rows(ht, size, gain[2:3, :])
    activate(ht, sh, mean, scale, bias[2:3, :])
    c_x.wait()
    c_r.wait()
    c_t.wait()

    turn_in(xv, xt)
    mean, scale = norm_rows(xt, size, gain[0:1, :])
    shift = 0.5 * bias[0:1, :]

    def body(start, _):
        y = silu_of_half((xt[pl.ds(start, CHUNK), :].astype(F32) - mean) * scale + shift)
        first[pl.ds(start, CHUNK), :] = y.astype(BF)
        return 0

    each_chunk(cells, body, 0)
    out_first = bring(first, first_hbm, 0)
    angle = step_ref[0].astype(F32) * rate[...]
    col = lax.broadcasted_iota(jnp.int32, angle.shape, 1)
    features = jnp.where(col < angle.shape[1] // 2, jnp.cos(angle), jnp.sin(angle))
    total = jnp.sum(jnp.dot(split3(features), tw[...], preferred_element_type=F32), axis=0, keepdims=True)
    tv[...] = total / (1.0 + jnp.exp(-total))
    out_tv = bring(tv, tv_hbm, 7)

    def tile(j, _):
        weights(j).wait()
        keep_far(j, far_tiles, conv_tile(sh, w[j]), me, far, mixed)
        return 0

    lax.fori_loop(0, far_tiles, tile, 0)
    out_far = bring(far.at[:, far_columns(me, channels)], far_hbm, 1)
    out_mixed = bring(mixed, mixed_hbm, 2)
    for c in (out_ht, out_tv, out_first, out_far, out_mixed):
        c.wait()


def stage_cover(me_ref, sh, w_hbm, near_hbm, w, near, sems, *, tiles):
    channels = w_hbm.shape[1]
    me = me_ref[0]
    far_tiles = -(-channels // WIDE)
    near_tiles = tiles - far_tiles

    def weights(j):
        return pltpu.make_async_copy(w_hbm.at[:, :, columns_of(me * far_tiles + j)], w.at[j], sems.at[j])

    def result(j):
        return pltpu.make_async_copy(
            near.at[:, columns_of(j)], near_hbm.at[:, columns_of(j)], sems.at[near_tiles + j])

    weights(0).start()

    def tile(j, _):
        weights(j).wait()

        @pl.when(j + 1 < near_tiles)
        def _():
            weights(j + 1).start()

        near[:, columns_of(j)] = conv_tile(sh, w[j])
        result(j).start()
        return 0

    lax.fori_loop(0, near_tiles, tile, 0)
    for j in range(near_tiles):
        result(j).wait()


def stage_middle(me_ref, mask_ref, got_ref, tvgot, cgot, own_hbm, tv_hbm, gain_hbm, bias_hbm, ut_hbm, ct_hbm, win_hbm,
                 wout_hbm, z_hbm, near_hbm, mixed_hbm, ht_hbm,
                 far_hbm, mix_hbm, sh, state,
                 xs, acc, xt, tv, gain, bias, ut, ct, win, wout, z, near, ht, far, mix, sems,
                 *, size, tiles):
    cells, channels = xt.shape
    full = xs.shape[1]
    me = me_ref[0]
    far_tiles = -(-channels // WIDE)
    near_wide = near_hbm.shape[1]
    start_tile = (1 - me) * (tiles - far_tiles)
    mine = pl.ds(pl.multiple_of(me * channels, LANES), channels)
    theirs = pl.ds(pl.multiple_of((1 - me) * channels, LANES), channels)
    places = (1, 0, 2)

    count = [0]

    def bring(src, dst):
        c = pltpu.make_async_copy(src, dst, sems.at[count[0]])
        count[0] += 1
        c.start()
        return c

    c_x = [bring(own_hbm, xs.at[pl.ds(S, cells), mine])]
    c_in = [bring(win_hbm.at[:, places[0]], win.at[0])]
    clear_border(xs)
    clear_border(sh)
    xs[S:S + cells, theirs] = got_ref[...]
    base = 17

    def out_weights(j):
        at = columns_of(start_tile + j)
        return (
            pltpu.make_async_copy(wout_hbm.at[:, :, at], wout.at[j], sems.at[base + 2 * j]),
            pltpu.make_async_copy(z_hbm.at[:, at], z.at[j], sems.at[base + 2 * j + 1]),
        )

    c_x[0].wait()
    c_in[0].wait()
    small = [bring(a, b) for a, b in ((tv_hbm, tv), (gain_hbm, gain), (bias_hbm, bias), (ut_hbm, ut), (ct_hbm, ct))]
    side = [
        bring(near_hbm, near.at[:, pl.ds(pl.multiple_of(me * LANES, LANES), near_wide)]),
        bring(mixed_hbm, near.at[:, pl.ds(pl.multiple_of((1 - me) * near_wide, LANES), LANES)]),
        bring(ht_hbm, ht),
    ]
    c_in.append(bring(win_hbm.at[:, places[1]], win.at[1]))

    def time_row(t_ref):
        a = lax.dot_general(split3(tv[...]), t_ref[:, mine], NT, preferred_element_type=F32)
        a = a + lax.dot_general(split3(tvgot[...]), t_ref[:, theirs], NT, preferred_element_type=F32)
        return jnp.sum(a, axis=0, keepdims=True)

    band = TILE * S
    where = lax.broadcasted_iota(jnp.int32, (band, LANES), 0) % S // TILE

    def gated_band(i, control_shift):
        rows = slice(i * band, (i + 1) * band)
        gate = jnp.zeros((band, LANES), F32)
        for t in range(S // TILE):
            gate = jnp.where(where == t, mask_ref[i, t].astype(F32), gate)
        for b in range(channels // LANES):
            part = slice(b * LANES, (b + 1) * LANES)
            value = near[rows, part] + cgot[rows, part].astype(F32) + ht[rows, part].astype(F32)
            state[rows, part] = ((value + control_shift[:, part]) * gate).astype(BF)

    bands = cells // band
    blocks = cells // WIDE
    col = lax.broadcasted_iota(jnp.int32, (channels, WIDE), 1) % S
    for s, place in enumerate(places):
        if s > 0:
            c_in[s].wait()
        if s == 1:
            for c in small + side:
                c.wait()
            control_shift = time_row(ct)
        weights = jnp.concatenate([win[s % 2, k] for k in range(3)], axis=1)
        for cb in range(blocks):
            rhs = jnp.concatenate([xs[S * dy + cb * WIDE:S * dy + cb * WIDE + WIDE, :] for dy in range(3)], axis=1)
            p = lax.dot_general(weights, rhs, NT, preferred_element_type=F32)
            part = slice(cb * WIDE, (cb + 1) * WIDE)
            if place == 1:
                acc[:, part] = p
            elif place == 0:
                acc[:, part] += jnp.where(col != 0, pltpu.roll(p, 1, 1), 0.0)
            else:
                acc[:, part] += jnp.where(col != S - 1, pltpu.roll(p, WIDE - 1, 1), 0.0)
            if s == 1:
                for i in range(cb * bands // blocks, (cb + 1) * bands // blocks):
                    gated_band(i, control_shift)
        if s == 0:
            c_in.append(bring(win_hbm.at[:, places[2]], win.at[0]))
            for j in range(far_tiles):
                for c in out_weights(j):
                    c.start()

    unet_shift = time_row(ut)
    for b in range(channels // LANES):
        part = slice(b * LANES, (b + 1) * LANES)
        xt[:, part] = (acc[part, :].T + unet_shift[:, part]).astype(BF)
    mean, scale = norm_rows(xt, size, gain[1:2, :])
    activate(xt, sh, mean, scale, bias[1:2, :])

    def tile(j, _):
        for c in out_weights(j):
            c.wait()
        keep_far(j, far_tiles, conv_tile(sh, wout[j], state[...], z[j]), me, far, mix)
        return 0

    lax.fori_loop(0, far_tiles, tile, 0)
    last = [bring(far.at[:, far_columns(me, channels)], far_hbm), bring(mix, mix_hbm)]
    for c in last:
        c.wait()


def stage_near(me_ref, sh, state, w_hbm, z_hbm, near, w, z, sems, *, tiles):
    channels = w_hbm.shape[1]
    me = me_ref[0]
    far_tiles = -(-channels // WIDE)
    near_tiles = tiles - far_tiles

    def weights(j):
        at = columns_of(me * far_tiles + j)
        return (
            pltpu.make_async_copy(w_hbm.at[:, :, at], w.at[j], sems.at[2 * j]),
            pltpu.make_async_copy(z_hbm.at[:, at], z.at[j], sems.at[2 * j + 1]),
        )

    for c in weights(0):
        c.start()

    def tile(j, _):
        for c in weights(j):
            c.wait()

        @pl.when(j + 1 < near_tiles)
        def _():
            for c in weights(j + 1):
                c.start()

        near[:, columns_of(j)] = conv_tile(sh, w[j], state[...], z[j])
        return 0

    lax.fori_loop(0, near_tiles, tile, 0)


def stage_last(me_ref, x_ref, near_ref, mixed_ref, got_ref, o_ref):
    b = pl.program_id(0)
    is_mixed = b == jnp.where(me_ref[0] == 0, pl.num_programs(0) - 1, 0)
    local = jnp.where(is_mixed, mixed_ref[...], near_ref[...])
    total = local + got_ref[...].astype(F32)
    o_ref[...] = (x_ref[...].astype(F32) + total.T).astype(BF)


def whole(shape):
    return pl.BlockSpec(shape, lambda *_: (0,) * len(shape), pipeline_mode=pl.Buffered(1))


def params(mib):
    return pltpu.CompilerParams(vmem_limit_bytes=mib << 20)


def far_off(*arrays):
    return [pltpu.with_memory_space_constraint(a, pltpu.HBM) for a in arrays]


def close(*arrays):
    return [pltpu.with_memory_space_constraint(a, pltpu.VMEM) for a in arrays]


def cost(flops, read):
    return pl.CostEstimate(flops=flops, bytes_accessed=read, transcendentals=0)


def local_pair(latent_x, control_h, tile_mask, timestep, time_weight, norm_gain, norm_bias, unet_conv_in,
               unet_conv_out, control_conv, unet_temb, control_temb, zero_conv):
    channels, cells = latent_x.shape
    full = unet_conv_in.shape[2]
    size = full // GROUPS
    swap = [(0, 1), (1, 0)]
    me = lax.axis_index("tensor").astype(jnp.int32).reshape(1)
    half_width = FREQ // 2
    rates = np.exp(-math.log(10000.0) * np.arange(half_width, dtype=np.float32) / half_width).astype(np.float32)
    rates = jnp.asarray(np.concatenate([rates, rates])[None, :])
    smem = pl.BlockSpec(memory_space=pltpu.SMEM)
    anywhere = pl.BlockSpec(memory_space=pl.ANY)
    vmem = pl.BlockSpec(memory_space=pltpu.VMEM)
    dma = pltpu.SemaphoreType.DMA
    tiles = full // WIDE
    far_tiles = -(-channels // WIDE)
    near_tiles = tiles - far_tiles
    taps = control_conv.shape[0]
    act = pltpu.HBM((cells, channels), BF)
    padded = pltpu.VMEM((cells + 2 * S, 3 * channels), BF)
    half_tile = pltpu.HBM((cells, LANES), F32)
    near_out = pltpu.HBM((cells, near_tiles * WIDE), F32)
    conv_flops = 2 * taps * channels * full * cells
    conv_bytes = 2 * taps * channels * full

    first, time_own, control_far, control_mixed, control_t, shifted = pl.pallas_call(
        functools.partial(stage_front, size=size, tiles=tiles),
        name="front",
        out_shape=(act, pltpu.HBM((1, channels), F32), act, half_tile, act, padded),
        in_specs=[smem, smem] + [anywhere] * 7,
        out_specs=(anywhere,) * 5 + (vmem,),
        scratch_shapes=[
            pltpu.VMEM((channels, cells), BF),
            pltpu.VMEM((channels, cells), BF),
            pltpu.VMEM((cells, channels), BF),
            pltpu.VMEM((cells, channels), BF),
            pltpu.VMEM(norm_gain.shape, F32),
            pltpu.VMEM(norm_bias.shape, F32),
            pltpu.VMEM(rates.shape, F32),
            pltpu.VMEM(time_weight.shape, BF),
            pltpu.VMEM((far_tiles, taps, channels, WIDE), BF),
            pltpu.VMEM((cells, channels), BF),
            pltpu.VMEM((1, channels), F32),
            pltpu.VMEM((cells, far_tiles * WIDE), BF),
            pltpu.VMEM((cells, LANES), F32),
            dma((8 + far_tiles,)),
        ],
        compiler_params=params(FRONT_MIB),
        cost_estimate=cost(conv_flops * far_tiles // tiles, conv_bytes * far_tiles // tiles),
    )(me, timestep, *far_off(latent_x, control_h, norm_gain, norm_bias, rates, time_weight, control_conv))
    first_got = lax.ppermute(first, "tensor", swap)
    time_got = lax.ppermute(time_own, "tensor", swap)
    control_got = lax.ppermute(control_far, "tensor", swap)

    control_near = pl.pallas_call(
        functools.partial(stage_cover, tiles=tiles),
        name="cover",
        out_shape=near_out,
        in_specs=[smem, vmem, anywhere],
        out_specs=anywhere,
        scratch_shapes=[
            pltpu.VMEM((near_tiles, taps, channels, WIDE), BF),
            pltpu.VMEM(near_out.shape, F32),
            dma((2 * near_tiles,)),
        ],
        compiler_params=params(COVER_MIB),
        cost_estimate=cost(conv_flops * near_tiles // tiles, conv_bytes * near_tiles // tiles),
    )(me, *close(shifted), *far_off(control_conv))

    mask = tile_mask.reshape(tile_mask.shape[1:])
    far, mixed, second, state = pl.pallas_call(
        functools.partial(stage_middle, size=size, tiles=tiles),
        name="middle",
        out_shape=(act, half_tile, padded, pltpu.VMEM((cells, channels), BF)),
        in_specs=[smem, smem, vmem, vmem, vmem] + [anywhere] * 12,
        out_specs=(anywhere, anywhere, vmem, vmem),
        scratch_shapes=[
            pltpu.VMEM((cells + 2 * S, full), BF),
            pltpu.VMEM((channels, cells), F32),
            pltpu.VMEM((cells, channels), BF),
            pltpu.VMEM((1, channels), F32),
            pltpu.VMEM(norm_gain.shape, F32),
            pltpu.VMEM(norm_bias.shape, F32),
            pltpu.VMEM(unet_temb.shape, BF),
            pltpu.VMEM(control_temb.shape, BF),
            pltpu.VMEM((2, 3, channels, full), BF),
            pltpu.VMEM((far_tiles, taps, channels, WIDE), BF),
            pltpu.VMEM((far_tiles, channels, WIDE), BF),
            pltpu.VMEM((cells, channels), F32),
            pltpu.VMEM((cells, channels), BF),
            pltpu.VMEM((cells, far_tiles * WIDE), BF),
            pltpu.VMEM((cells, LANES), F32),
            dma((17 + 2 * far_tiles,)),
        ],
        compiler_params=params(MIDDLE_MIB),
        cost_estimate=cost(conv_flops * (tiles + far_tiles) // tiles, conv_bytes * (tiles + far_tiles) // tiles),
    )(me, mask, *close(first_got, time_got, control_got),
      *far_off(first, time_own, norm_gain, norm_bias, unet_temb, control_temb,
               unet_conv_in.reshape(3, 3, channels, full), unet_conv_out, zero_conv, control_near,
               control_mixed, control_t))
    got = lax.ppermute(far, "tensor", swap)

    near = pl.pallas_call(
        functools.partial(stage_near, tiles=tiles),
        name="near",
        out_shape=pltpu.VMEM(near_out.shape, F32),
        in_specs=[smem, vmem, vmem, anywhere, anywhere],
        out_specs=vmem,
        scratch_shapes=[
            pltpu.VMEM((near_tiles, taps, channels, WIDE), BF),
            pltpu.VMEM((near_tiles, channels, WIDE), BF),
            dma((2 * near_tiles,)),
        ],
        compiler_params=params(COVER_MIB),
        cost_estimate=cost(conv_flops * near_tiles // tiles, conv_bytes * near_tiles // tiles),
    )(me, *close(second, state), *far_off(unet_conv_out, zero_conv))

    last_near = near_tiles * WIDE // LANES - 1
    return pl.pallas_call(
        stage_last,
        name="last",
        out_shape=jax.ShapeDtypeStruct((channels, cells), BF),
        grid_spec=pltpu.PrefetchScalarGridSpec(
            num_scalar_prefetch=1,
            grid=(channels // LANES,),
            in_specs=[
                pl.BlockSpec((LANES, cells), lambda b, i: (b, 0)),
                pl.BlockSpec((cells, LANES), lambda b, i: (0, jnp.clip(b - i[0], 0, last_near))),
                whole((cells, LANES)),
                pl.BlockSpec((cells, LANES), lambda b, i: (0, b)),
            ],
            out_specs=pl.BlockSpec((LANES, cells), lambda b, i: (b, 0)),
        ),
        compiler_params=params(LAST_MIB),
        cost_estimate=cost(4 * channels * cells, 10 * channels * cells),
    )(me, latent_x, near, mixed, got)


def norm_silu(inputs, scales, shifts):
    rows_count = inputs.shape[0]
    group_size = C // GROUPS
    grouped = inputs.astype(jnp.float32).reshape(rows_count // group_size, group_size, VIEWS, S * S)
    average = jnp.mean(grouped, axis=(1, 3), keepdims=True)
    centred = grouped - average
    variance = jnp.mean(centred * centred, axis=(1, 3), keepdims=True)
    normed = (centred * lax.rsqrt(variance + 1e-05)).reshape(rows_count, VIEWS * S * S)
    return jax.nn.silu(normed * scales[:, None] + shifts[:, None]).astype(jnp.bfloat16)


def tap_mask(place, cells):
    where = jnp.arange(cells, dtype=jnp.int32)
    row_index = where // S % S + (place // 3 - 1)
    col_index = where % S + (place % 3 - 1)
    inside = (row_index >= 0) & (row_index < S) & (col_index >= 0) & (col_index < S)
    return inside.astype(jnp.float32)


def shift_cells(values, place):
    cells = values.shape[1]
    offset_cells = (place // 3 - 1) * S + (place % 3 - 1)
    padded = jnp.pad(values, ((0, 0), (S + 1, S + 1)))
    moved = lax.slice_in_dim(padded, S + 1 + offset_cells, S + 1 + offset_cells + cells, axis=1)
    return moved * tap_mask(place, cells)[None, :]


def conv_plain(weights, inputs, running):
    for place in range(9):
        product = jnp.dot(weights[place], inputs, preferred_element_type=jnp.float32)
        running = running + shift_cells(product, place)
    return running


def conv_flipped(weights, inputs):
    running = None
    for place in range(9):
        product = lax.dot_general(
            weights[place], inputs, (((0,), (0,)), ((), ())), preferred_element_type=jnp.float32
        )
        moved = shift_cells(product, place)
        running = moved if running is None else running + moved
    return running


def expand_mask(tile_mask):
    blocks = tile_mask.astype(jnp.float32)[:, :, None, :, None]
    spread_mask = jnp.broadcast_to(blocks, (VIEWS, S // TILE, TILE, S // TILE, TILE))
    return spread_mask.reshape(VIEWS * S * S)


def local_any(
    latent_x,
    control_h,
    tile_mask,
    timestep,
    time_weight,
    norm_gain,
    norm_bias,
    unet_conv_in,
    unet_conv_out,
    control_conv,
    unet_temb,
    control_temb,
    zero_conv,
):
    local_time = jax.nn.silu(
        jnp.dot(
            timestep_features(timestep),
            time_weight.astype(jnp.float32),
            precision=lax.Precision.HIGHEST,
        )
    )
    time_vector = lax.all_gather(local_time, "tensor", axis=0, tiled=True)
    unet_shift = jnp.dot(
        unet_temb.astype(jnp.float32), time_vector, precision=lax.Precision.HIGHEST
    )
    control_shift = jnp.dot(
        control_temb.astype(jnp.float32), time_vector, precision=lax.Precision.HIGHEST
    )
    gate_row = expand_mask(tile_mask)
    channels = latent_x.shape[0]
    first = norm_silu(latent_x, norm_gain[0], norm_bias[0])
    initial = jnp.zeros((channels, latent_x.shape[1]), jnp.float32)
    weights = unet_conv_in
    hidden_sum = conv_plain(weights, lax.all_gather(first, "tensor", axis=0, tiled=True), initial)
    hidden = (hidden_sum + unet_shift[:, None]).astype(jnp.bfloat16)
    hidden = lax.optimization_barrier(hidden)
    second = norm_silu(hidden, norm_gain[1], norm_bias[1])
    control_act = norm_silu(control_h, norm_gain[2], norm_bias[2])
    weights = control_conv
    control_sum = lax.psum_scatter(
        conv_flipped(weights, control_act).astype(jnp.bfloat16),
        "tensor",
        scatter_dimension=0,
        tiled=True,
    ).astype(jnp.float32)
    control_state = (control_h.astype(jnp.float32) + control_sum + control_shift[:, None]).astype(
        jnp.bfloat16
    )
    weights = zero_conv
    product = lax.dot_general(
        weights, control_state, (((0,), (0,)), ((), ())), preferred_element_type=jnp.float32
    )
    weights = unet_conv_out
    combined = lax.psum_scatter(
        (conv_flipped(weights, second) + product * gate_row[None, :]).astype(jnp.bfloat16),
        "tensor",
        scatter_dimension=0,
        tiled=True,
    ).astype(jnp.float32)
    return (latent_x.astype(jnp.float32) + combined).astype(jnp.bfloat16)


def solution(mesh):
    placed = (
        P("tensor", "dp"),
        P("tensor", "dp"),
        P("dp", None, None),
        P("dp"),
        P(None, "tensor"),
        P(None, "tensor"),
        P(None, "tensor"),
        P(None, "tensor", None),
        P(None, "tensor", None),
        P(None, "tensor", None),
        P("tensor", None),
        P("tensor", None),
        P("tensor", None),
    )

    def local(latent_x, *rest):
        channels, cells = latent_x.shape
        paired = mesh.shape["tensor"] == 2 and channels % WIDE == LANES and VIEWS == 1 and cells == S * S
        return (local_pair if paired else local_any)(latent_x, *rest)

    return jax.shard_map(
        local, mesh=mesh, in_specs=placed, out_specs=P("tensor", "dp"), check_vma=False
    )
```
